32 devices in a mesh: lat: 4 (over z), lon: 8 (over y, x, core).
Axes of the slice: x: 2, y: 2, z: 4, core: 2. Of those that a mesh axis runs over, the one named last changes fastest.
Arguments:
- state: bfloat16 [192, 64, 1024], P(None, 'lat', 'lon'), may hold values from -6 to 6
- depth_kernel: bfloat16 [192, 7, 7], replicated, may hold values from -0.875 to 0.875
- point_weight: bfloat16 [192, 192], replicated, may hold values from -0.4375 to 0.4375
- column_index: int32 [16384, 4], P(('lat', 'lon')), may hold values from 0 to 2047, as said below
- column_weight: bfloat16 [16384, 4], P(('lat', 'lon')), may hold values from 0.049804688 to 0.59765625
- owner: int32 [16384, 1], P(('lat', 'lon')), may hold values from 0 to 7; in each aligned block of 512 rows (0 to 511, 512 to 1023, ...) at most 64 rows name the same one
- observed: bfloat16 [16384, 137], P(('lat', 'lon')), may hold values from -6 to 6
- hidden_weight: bfloat16 [8, 192, 512], P('lon'), may hold values from -0.4375 to 0.4375
- level_weight: bfloat16 [8, 512, 137], P('lon'), may hold values from -0.25 to 0.25
- inverse_error: bfloat16 [8, 137], P('lon'), may hold values from 0.25 to 4
Outputs:
- gradient: bfloat16 [192, 64, 1024], P(None, 'lat', 'lon')
- departures: bfloat16 [16384, 137], P(('lat', 'lon'))
The draws below stay inside these ranges and needn't reach their ends.
Inputs may be any that keep to these rules, and one draw needn't show every extreme that they name: `column_index`: the four columns of one grid box of the sounding's own tile: b, b + 1, b + 128, b + 129. `owner`: among the 512 soundings of one tile no instrument appears more than 64 times.
All inputs are finite; a program needn't handle non-finite values.
Results may differ from the reference program's by a relative error of at most 0.0085.
Values may be sent and summed in bfloat16 or wider, within the bound.
A program may use at most 128 MiB of HBM per device.

```python
import math
import jax
import jax.numpy as jnp
import numpy as np
from jax import lax

C = 192
HID = 512
LEV = 137
TLAT = 16
TLON = 128
OBS_DEV = 512
CAP = 64
NLAT = 64
NLON = 1024
NSOUND = 16384
N_LAT = 4
N_LON = 8


def draw_column_index(key, part):
    base_lat = jax.random.randint(jax.random.fold_in(key, 11), (NSOUND, 1), 0, TLAT - 1)
    base_lon = jax.random.randint(jax.random.fold_in(key, 23), (NSOUND, 1), 0, TLON - 1)
    corner = base_lat * TLON + base_lon
    offsets = jnp.array([0, 1, TLON, TLON + 1], dtype=jnp.int32)
    return (corner + offsets[None, :]).astype(jnp.int32)


def block_levels(rng, extent, pieces, low, high):
    gain = 1.0
    for position, shards_of in pieces:
        draws = jax.random.uniform(jax.random.fold_in(jax.random.fold_in(rng, 6), position), (shards_of,), jnp.float32, low / len(pieces), high / len(pieces))
        gain = gain * jnp.repeat(jnp.exp(draws), extent[position] // shards_of).reshape((-1,) + (1,) * (len(extent) - 1 - position))
    return gain


def routed_block(key, own, number, rows, amount, top, bound, slope):
    ranking = jax.random.permutation(key, amount)
    packed, common = load_shares(amount, rows * top, bound, slope, True), load_shares(amount, rows * top, bound, slope, False)
    places = jnp.arange(amount)

    def named(sizes, turn):
        used = int((sizes > 0).sum())
        fixed = max(1, used // 4)
        passed = fixed + (places - fixed + turn * (used - fixed)) % max(1, amount - fixed)
        return jnp.zeros((amount,), jnp.int32).at[ranking[jnp.where(places < fixed, places, passed)]].set(jnp.asarray(sizes, jnp.int32))

    sizes = jnp.where(number % 4 == 0, named(packed, number // 4), named(common, number - number // 4 - 1))
    mixed = jax.random.permutation(jax.random.fold_in(own, 3), amount)
    donor, taker = mixed[0:amount // 2 * 2:2], mixed[1:amount // 2 * 2:2]
    margin = jnp.minimum(sizes[donor] - 1, bound - sizes[taker]) // 2
    margin = jnp.where((donor == ranking[0]) | (taker == ranking[0]) | (sizes[taker] == 0), 0, jnp.maximum(margin, 0))
    passed = jax.random.randint(jax.random.fold_in(own, 4), (amount // 2,), 0, 1 << 20) % (margin + 1)
    sizes = sizes.at[donor].add(-passed).at[taker].add(passed)
    labels = jnp.searchsorted(jnp.cumsum(sizes), jnp.arange(rows * top), side="right").astype(jnp.int32)
    listing = labels.reshape(top, rows).T
    listing = listing[jax.random.permutation(jax.random.fold_in(own, 1), rows)]
    turn = jax.random.randint(jax.random.fold_in(own, 2), (rows, 1), 0, top)
    return jnp.take_along_axis(listing, (jnp.arange(top)[None, :] + turn) % top, axis=1)


def load_shares(number_of, total, reach, skew, full):
    portions = [(1 << 20) // math.isqrt(rank ** skew) + 1 for rank in range(1, number_of + 1)]
    largest = reach if full else min(reach, max(-(-total // number_of), total * portions[0] // sum(portions)))
    least = 1 if total - largest >= number_of - 1 else 0
    counts, rest = [largest] + [least] * (number_of - 1), total - largest - least * (number_of - 1)
    while rest > 0:
        free = [i for i in range(1, number_of) if counts[i] < largest] or [i for i in range(1, number_of) if counts[i] < reach]
        pool, remaining = sum([portions[i] for i in free]), rest
        for i in free:
            extra = min(reach - counts[i], max(1, remaining * portions[i] // pool), rest)
            counts[i] = counts[i] + extra
            rest = rest - extra
    return np.array(counts)


def gaussian(key, extent, width, most, shards=(), held_as=jnp.bfloat16):
    level = block_levels(key, extent, shards, -0.22, 0.18) if shards else 1.0
    values = jax.random.normal(key, extent, jnp.float32) * width * level
    return jnp.minimum(jnp.maximum(values, -most), most).astype(held_as)


def setup_inputs(seed: int = 0) -> dict:
    keys = jax.random.split(jax.random.key(seed), 11)
    state = gaussian(keys[0], (C, NLAT, NLON), 1.0, 6.0, ((1, 4), (2, 8)))
    depth_kernel = gaussian(keys[1], (C, 7, 7), 49 ** -0.5, 0.875)
    point_weight = gaussian(keys[2], (C, C), C ** -0.5, 0.4375)
    column_index = draw_column_index(jax.random.fold_in(keys[10], 71), 0)
    column_weight = jnp.clip(0.049804688 + 0.54785156 * jax.random.uniform(keys[4], (NSOUND, 4), jnp.float32) ** block_levels(keys[4], (NSOUND, 4), ((0, 32),), -0.2, 0.2), 0.049804688, 0.59765625).astype(jnp.bfloat16)
    owner_keys = jax.random.split(jax.random.fold_in(keys[5], 1), NSOUND // OBS_DEV)
    owner_turns = jax.random.permutation(jax.random.fold_in(keys[5], 3), NSOUND // OBS_DEV)
    owner = jax.vmap(lambda own, number: routed_block(jax.random.fold_in(keys[5], 2), own, number, OBS_DEV, N_LON, 1, CAP, 2))(owner_keys, owner_turns).reshape((NSOUND, 1))
    observed = gaussian(keys[6], (NSOUND, LEV), 1.0, 6.0, ((0, 32),))
    hidden_weight = gaussian(keys[7], (N_LON, C, HID), C ** -0.5, 0.4375, ((0, 8),))
    level_weight = gaussian(keys[8], (N_LON, HID, LEV), HID ** -0.5, 0.25, ((0, 8),))
    inverse_error = jnp.clip(jnp.exp(math.log(4.0) - 2.7725887 * jax.random.uniform(keys[9], (N_LON, LEV), jnp.float32) ** block_levels(keys[9], (N_LON, LEV), ((0, 8),), -0.2, 0.2)), 0.25, 4.0).astype(jnp.bfloat16)
    return dict(state=state, depth_kernel=depth_kernel, point_weight=point_weight, column_index=column_index, column_weight=column_weight, owner=owner, observed=observed, hidden_weight=hidden_weight, level_weight=level_weight, inverse_error=inverse_error)


def rounded(values):
    return lax.optimization_barrier(values.astype(jnp.bfloat16))

def pad_grid(values):
    values = jnp.pad(values, ((0, 0), (3, 3), (0, 0)))
    return jnp.pad(values, ((0, 0), (0, 0), (3, 3)), mode='wrap')

def depthwise(values, kernel):
    height = values.shape[1]
    breadth = values.shape[2]
    padded = pad_grid(values)

    def one_channel(pair):
        plane, weights_c = pair
        weights_c = weights_c.astype(jnp.float32)
        summed = jnp.zeros((height, breadth), jnp.float32)
        for row_tap in range(7):
            for col_tap in range(7):
                summed = summed + weights_c[row_tap, col_tap] * plane[row_tap:row_tap + height, col_tap:col_tap + breadth].astype(jnp.float32)
        return summed
    return lax.map(one_channel, (padded, kernel))

def observe(profiles, observed, hidden_w, level_w, inverse_e):
    pre_act = jnp.dot(profiles, hidden_w, preferred_element_type=jnp.float32)
    squashed = jnp.tanh(pre_act)
    levels = jnp.dot(rounded(squashed), level_w, preferred_element_type=jnp.float32)
    misfit = levels - observed.astype(jnp.float32)
    weighted = rounded(inverse_e.astype(jnp.float32)[None, :] * misfit)
    back_hidden = jnp.dot(weighted, level_w.T, preferred_element_type=jnp.float32)
    back_pre = rounded(back_hidden * (1.0 - squashed * squashed))
    adjoint = jnp.dot(back_pre, hidden_w.T, preferred_element_type=jnp.float32)
    return (adjoint.astype(jnp.bfloat16), misfit.astype(jnp.bfloat16))

def reference(state, depth_kernel, point_weight, column_index, column_weight, owner, observed, hidden_weight, level_weight, inverse_error):
    devices_n = N_LAT * N_LON
    cells = NLAT * NLON
    mixed = rounded(depthwise(state, depth_kernel)).reshape(C, cells)
    pre_gelu = jnp.dot(point_weight.T, mixed, preferred_element_type=jnp.float32)
    analysis = rounded(state.reshape(C, cells).astype(jnp.float32) + jax.nn.gelu(pre_gelu))
    device = jnp.arange(NSOUND, dtype=jnp.int32) // OBS_DEV
    tile_lat = device // N_LON
    tile_lon = device % N_LON
    local_lat = column_index // TLON
    local_lon = column_index % TLON
    global_index = ((tile_lat[:, None] * TLAT + local_lat) * NLON + tile_lon[:, None] * TLON + local_lon).astype(jnp.int32)
    weights_f = column_weight.astype(jnp.float32)
    profile_t = jnp.zeros((C, NSOUND), jnp.float32)
    for corner in range(4):
        profile_t = profile_t + analysis[:, global_index[:, corner]].astype(jnp.float32) * weights_f[:, corner][None, :]
    profiles = profile_t.T.astype(jnp.bfloat16)
    sounding = owner[:, 0].reshape(devices_n, OBS_DEV)
    onehot = (sounding[:, :, None] == jnp.arange(N_LON, dtype=jnp.int32)[None, None, :]).astype(jnp.int32)
    before = jnp.cumsum(onehot, axis=1) - onehot
    within = lax.optimization_barrier(jnp.sum(before * onehot, axis=2))
    slot_of = (sounding * CAP + within).astype(jnp.int32)
    device_ids = jnp.broadcast_to(jnp.arange(devices_n, dtype=jnp.int32)[:, None], (devices_n, OBS_DEV))
    buffer_prof = jnp.zeros((devices_n, N_LON * CAP, C), jnp.bfloat16).at[device_ids, slot_of].set(profiles.reshape(devices_n, OBS_DEV, C))
    buffer_obs = jnp.zeros((devices_n, N_LON * CAP, LEV), jnp.bfloat16).at[device_ids, slot_of].set(observed.reshape(devices_n, OBS_DEV, LEV))
    by_instrument_prof = buffer_prof.reshape(devices_n, N_LON, CAP, C).transpose(1, 0, 2, 3).reshape(N_LON, devices_n * CAP, C)
    by_instrument_obs = buffer_obs.reshape(devices_n, N_LON, CAP, LEV).transpose(1, 0, 2, 3).reshape(N_LON, devices_n * CAP, LEV)

    def per_instrument(group):
        return observe(group[0], group[1], group[2], group[3], group[4])
    adjoint_all, misfit_all = lax.map(per_instrument, (by_instrument_prof, by_instrument_obs, hidden_weight, level_weight, inverse_error))
    adjoint_all = adjoint_all.reshape(N_LON, devices_n, CAP, C).transpose(1, 0, 2, 3).reshape(devices_n, N_LON * CAP, C)
    misfit_all = misfit_all.reshape(N_LON, devices_n, CAP, LEV).transpose(1, 0, 2, 3).reshape(devices_n, N_LON * CAP, LEV)
    adjoint_profiles = adjoint_all[device_ids, slot_of].reshape(NSOUND, C)
    departures = misfit_all[device_ids, slot_of].reshape(NSOUND, LEV)
    adjoint_f = adjoint_profiles.astype(jnp.float32)
    feedback = jnp.zeros((C, cells), jnp.float32)
    for corner in range(4):
        feedback = feedback.at[:, global_index[:, corner]].add((adjoint_f * weights_f[:, corner][:, None]).T)
    unused, pull_back = jax.vjp(jax.nn.gelu, pre_gelu)
    gate_back = pull_back(feedback)[0].astype(jnp.bfloat16)
    mixed_back = rounded(jnp.dot(point_weight, gate_back, preferred_element_type=jnp.float32)).reshape(C, NLAT, NLON)
    spread_back = depthwise(mixed_back, depth_kernel[:, ::-1, ::-1])
    gradient = (feedback.reshape(C, NLAT, NLON) + spread_back).astype(jnp.bfloat16)
    return (gradient, departures)
```

```python
import jax
import jax.numpy as jnp
from jax import lax
from jax.experimental import pallas as pl
from jax.experimental.pallas import tpu as pltpu
from jax.sharding import PartitionSpec as P

CAP = 64
F32 = jnp.float32
BF = jnp.bfloat16
VM = pl.BlockSpec(memory_space=pltpu.VMEM)


def nn(a, b):
    return jnp.dot(a, b, preferred_element_type=F32)


def nt(a, b):
    return lax.dot_general(a, b, (((1,), (1,)), ((), ())), preferred_element_type=F32)


def flip_bit(q, bit):
    return q + bit * (1 - 2 * lax.rem(q // bit, 2))


def shifted(v, shift):
    breadth = v.shape[1]
    if not shift:
        return v
    lane = lax.broadcasted_iota(jnp.int32, v.shape, 1)
    keep = lane < breadth - shift if shift > 0 else lane >= -shift
    return jnp.where(keep, pltpu.roll(v, (-shift) % breadth, 1), jnp.zeros_like(v))


def build_rows(taps, flip, height, breadth, a_ref):
    depth, width = taps.shape[1], 2 * breadth
    lane = lax.broadcasted_iota(jnp.int32, (1, width), 1)
    tap = lax.broadcasted_iota(jnp.int32, (depth, width), 0)
    own_col, own_row = lane // height, lane % height
    q = lane - breadth
    edge_col, k = q // 8, q % 8
    edge_row = jnp.where(k < 4, k - 3, height + k - 4)
    is_own = lane < 7 * height
    is_edge = (q >= 0) & (q < 56) & (k != 3) & (k != 7)
    col = jnp.where(is_own, own_col, edge_col)
    row = jnp.where(is_own, own_row, edge_row)

    def one(i, carry):
        a = row - i + 3
        good = (is_own | is_edge) & (a >= 0) & (a < 7)
        want = (6 - a) * 8 + 6 - col if flip else a * 8 + col
        want = jnp.where(good, want, -1)
        pick = jnp.where(tap == want, 1.0, 0.0).astype(BF)
        rows = nn(taps, pick)
        for t in range(2):
            a_ref[t, pl.ds(i, taps.shape[0], stride=height), :] = rows[
                :, t * breadth : (t + 1) * breadth
            ]
        return carry

    lax.fori_loop(0, height, one, 0)


def side_weights(k_ref, flip, w_ref):
    channels = k_ref.shape[2]
    slot = lax.broadcasted_iota(jnp.int32, (8, channels), 0)
    for a in range(7):
        taps = k_ref[6 - a if flip else a].astype(F32)
        for d in range(3):
            r, l = (d, 6 - d) if flip else (6 - d, d)
            right = jnp.where(slot >= 5 + d, jnp.broadcast_to(taps[r : r + 1], slot.shape), 0.0)
            left = jnp.where(slot <= 2 - d, jnp.broadcast_to(taps[l : l + 1], slot.shape), 0.0)
            w_ref[a * 3 + d] = right + left


def conv_own(load, a_ref, out, height, breadth, count):
    def pair(p, carry):
        at = pl.ds(pl.multiple_of(p * 2 * height, 2 * height), 2 * height)
        both = load(p, at)
        cols = [
            jnp.concatenate([shifted(v, b - 3) for b in range(7)], axis=0) for v in both
        ]
        lhs = a_ref[0, at, : 7 * height].astype(BF)
        got = nn(lhs, jnp.concatenate(cols, axis=1))
        for e in range(2):
            rows = pl.ds(pl.multiple_of((p * 2 + e) * height, height), height)
            out[rows, :] = got[e * height : (e + 1) * height, e * breadth : (e + 1) * breadth]
        return carry

    lax.fori_loop(0, count, pair, 0, unroll=4)


def conv_edge(hal, a_ref, p, height, breadth):
    cols = []
    for e in range(2):
        v = hal[pl.ds(pl.multiple_of((p * 2 + e) * 8, 8), 8), :]
        cols.append(
            jnp.concatenate([shifted(v, b - 3) for b in range(7)], axis=0).astype(BF)
        )
    at = pl.ds(pl.multiple_of(p * 2 * height, 2 * height), 2 * height)
    lhs = a_ref[1, at, :56].astype(BF)
    got = nn(lhs, jnp.concatenate(cols, axis=1))
    return [
        got[e * height : (e + 1) * height, e * breadth : (e + 1) * breadth] for e in range(2)
    ]


def side_sum(right_in, left_in, w_ref, m_ref, c_ref, ct_ref):
    rows, _, channels = right_in.shape
    height = rows - 6
    slot = lax.broadcasted_iota(jnp.int32, (8, channels), 0)

    def turn(r, carry):
        both = jnp.where(slot < 4, right_in[r].astype(F32), left_in[r].astype(F32))
        for d in range(3):
            m_ref[d, r] = jnp.where(
                slot >= 5, pltpu.roll(both, 5 + d, 0), pltpu.roll(both, 3 - d, 0)
            )
        return carry

    lax.fori_loop(0, rows, turn, 0, unroll=2)

    def group(g, carry):
        acc = [jnp.zeros((8, channels), F32) for _ in range(4)]
        for d in range(3):
            for a in range(7):
                w = w_ref[a * 3 + d]
                for i in range(4):
                    acc[i] = acc[i] + w * m_ref[d, g * 4 + i + a]
        for i in range(4):
            c_ref[pl.ds(pl.multiple_of((g * 4 + i) * 8, 8), 8), :] = acc[i]
        return carry

    lax.fori_loop(0, height // 4, group, 0)
    ct_ref[...] = c_ref[...].T.astype(BF)


def side_place(i, height, breadth):
    part = lax.broadcasted_iota(jnp.int32, (8 * height, breadth), 0)
    lane = lax.broadcasted_iota(jnp.int32, (8 * height, breadth), 1)
    s = part - i * 8
    hit = ((s >= 0) & (s < 3) & (lane == s)) | ((s > 4) & (s < 8) & (lane == s + breadth - 8))
    return jnp.where(hit, 1.0, 0.0).astype(BF)


def take_rows(lat_in, hal, channels):
    for t in range(2):
        for k in range(3):
            hal[pl.ds(4 * t + k, channels, stride=8), :] = lat_in[t, k].astype(F32)


def prepare(owner, index, weight, obs_t, meta, wt_ref, p_ref, pt_ref, obs_slot, height, breadth):
    obs = wt_ref.shape[0]
    slots = p_ref.shape[0]
    n = slots // CAP
    si = lax.broadcasted_iota(jnp.int32, (obs, obs), 0)
    sj = lax.broadcasted_iota(jnp.int32, (obs, obs), 1)
    earlier = jnp.where(si < sj, 1.0, 0.0).astype(BF)
    own = owner[...]
    hot = jnp.where(lax.broadcasted_iota(jnp.int32, (n, obs), 0) == own, 1.0, 0.0)
    within = jnp.sum(nn(hot.astype(BF), earlier) * hot, axis=0, keepdims=True)
    slot_row = own * CAP + within.astype(jnp.int32)
    corner = index[0:1, :].astype(F32)
    row0 = jnp.floor((corner + 0.5) / breadth)
    meta[...] = jnp.zeros_like(meta)
    meta[0:4, :] = weight[...].astype(F32)
    meta[4:5, :] = row0
    meta[5:6, :] = corner - row0 * breadth
    meta[6:7, :] = slot_row.astype(F32)
    by_obs = meta[...].T
    w = by_obs[:, 0:4]
    whole = by_obs.astype(jnp.int32)
    lane = lax.broadcasted_iota(jnp.int32, (obs, breadth), 1)
    r0 = jnp.broadcast_to(whole[:, 4:5], (obs, breadth))
    c0 = jnp.broadcast_to(whole[:, 5:6], (obs, breadth))
    zero = jnp.zeros((obs, breadth), F32)
    first = lane == c0
    second = lane == c0 + 1
    top = jnp.where(first, w[:, 0:1], jnp.where(second, w[:, 1:2], zero))
    bottom = jnp.where(first, w[:, 2:3], jnp.where(second, w[:, 3:4], zero))
    for r in range(height):
        wt_ref[:, r * breadth : (r + 1) * breadth] = jnp.where(r0 == r, top, jnp.where(r0 == r - 1, bottom, zero)).astype(BF)
    place = lax.broadcasted_iota(jnp.int32, (slots, obs), 0) == slot_row
    p = jnp.where(place, 1.0, 0.0).astype(BF)
    p_ref[...] = p
    place = lax.broadcasted_iota(jnp.int32, (obs, slots), 1) == whole[:, 6:7]
    pt_ref[...] = jnp.where(place, 1.0, 0.0).astype(BF)
    obs_slot[...] = nt(p, obs_t[...]).astype(BF)


def remote(src, dst, send, recv, device):
    return pltpu.make_async_remote_copy(
        src_ref=src,
        dst_ref=dst,
        send_sem=send,
        recv_sem=recv,
        device_id=device,
        device_id_type=pl.DeviceIdType.MESH,
    )


def selector(breadth):
    s = lax.broadcasted_iota(jnp.int32, (8, breadth), 0)
    lane = lax.broadcasted_iota(jnp.int32, (8, breadth), 1)
    near = (s < 3) & (lane == s)
    far = (s > 4) & (lane == s + (breadth - 8))
    return jnp.where(near | far, 1.0, 0.0).astype(BF)


def copies(lat_out, lat_in, edge, right_in, left_in, send, recv, lats, lons):
    height = edge.shape[0]
    lat, lon = lax.axis_index("lat"), lax.axis_index("lon")
    left, right = lax.rem(lon + lons - 1, lons), lax.rem(lon + 1, lons)
    low, high, mid = pl.ds(0, 3), pl.ds(height + 3, 3), pl.ds(3, height)
    end = pl.ds(height - 3, 3)

    def make(i, a, b, device):
        return remote(a, b, send.at[i], recv.at[i], device)

    side = [
        make(2, edge, right_in.at[mid], {"lat": lat, "lon": left}),
        make(3, edge, left_in.at[mid], {"lat": lat, "lon": right}),
    ]
    u, d = lax.max(lat - 1, 0), lax.min(lat + 1, lats - 1)
    up = [
        make(0, lat_out.at[0], lat_in.at[1], {"lat": u, "lon": lon}),
        make(4, edge.at[low], right_in.at[high], {"lat": u, "lon": left}),
        make(5, edge.at[low], left_in.at[high], {"lat": u, "lon": right}),
    ]
    down = [
        make(1, lat_out.at[1], lat_in.at[0], {"lat": d, "lon": lon}),
        make(6, edge.at[end], right_in.at[low], {"lat": d, "lon": left}),
        make(7, edge.at[end], left_in.at[low], {"lat": d, "lon": right}),
    ]
    return lat > 0, lat < lats - 1, up, down, side


def start_lat(lat_out, lat_in, edge, right_in, left_in, send, recv, lats, lons):
    height = edge.shape[0]
    has_up, has_down, up, down, side = copies(
        lat_out, lat_in, edge, right_in, left_in, send, recv, lats, lons
    )

    @pl.when(has_up)
    def _():
        for copy in up:
            copy.start()

    @pl.when(has_down)
    def _():
        for copy in down:
            copy.start()

    for has, t, at in ((has_up, 0, 0), (has_down, 1, height + 3)):

        @pl.when(jnp.logical_not(has))
        def _():
            lat_in[t] = jnp.zeros(lat_in.shape[1:], BF)
            for ref in (right_in, left_in):
                ref[at : at + 3] = jnp.zeros((3,) + ref.shape[1:], BF)


def start_side(*refs):
    for copy in copies(*refs)[4]:
        copy.start()


def end_exchange(*refs):
    has_up, has_down, up, down, side = copies(*refs)

    @pl.when(has_up)
    def _():
        for copy in down:
            copy.wait_recv()
        for copy in up:
            copy.wait_send()

    @pl.when(has_down)
    def _():
        for copy in up:
            copy.wait_recv()
        for copy in down:
            copy.wait_send()

    for copy in side:
        copy.wait()


def kernel(
    lats,
    lons,
    state,
    hw_ref,
    lw_ref,
    err_ref,
    owner,
    index,
    weight,
    obs_t,
    k_ref,
    pw_ref,
    out_ref,
    dep_ref,
    cells,
    back,
    part,
    a1,
    a2,
    w1,
    w2,
    m_sc,
    c_sc,
    ct_sc,
    hal,
    lat_out,
    lat_in,
    meta,
    tap_rows,
    taps,
    pwt,
    edge,
    right_in,
    left_in,
    ops,
    wt,
    p_mat,
    pt_mat,
    obs_slot,
    grid_f,
    ana,
    prof,
    adj,
    mis,
    send,
    recv,
    op_send,
    op_recv,
):
    channels, height, breadth = state.shape
    levels = obs_t.shape[0]
    err_row = ops.shape[1] - 16
    lat, lon = lax.axis_index("lat"), lax.axis_index("lon")
    partner = lon + 1 - 2 * lax.rem(lon, 2)
    other = lax.rem(lon + lons - 1 + 2 * lax.rem(lon, 2), lons)
    half = lons // 2
    peers = [lax.rem(lon + 2 * j, lons) for j in range(1, half)]
    barrier = pltpu.get_barrier_semaphore()

    def greet(a, b):
        pl.semaphore_signal(
            barrier,
            inc=1,
            device_id={"lat": a, "lon": b},
            device_id_type=pl.DeviceIdType.MESH,
        )

    for b in [partner, other] + peers:
        greet(lat, b)

    @pl.when(lat > 0)
    def _():
        for b in (partner, lon, other):
            greet(lat - 1, b)

    @pl.when(lat < lats - 1)
    def _():
        for b in (partner, lon, other):
            greet(lat + 1, b)

    cells[...] = state[...].reshape(channels * height, breadth).astype(F32)

    def wires(k):
        return (
            lat_out.at[k],
            lat_in.at[k],
            edge.at[k],
            right_in.at[k],
            left_in.at[k],
            send.at[k],
            recv.at[k],
            lats,
            lons,
        )

    def row_of(ref, r):
        return ref[pl.ds(r, channels, stride=height), :]

    pick = selector(breadth)

    def edge_row(r, carry):
        edge[0, r] = nt(pick, row_of(cells, r).astype(BF)).astype(BF)
        return carry

    lax.fori_loop(0, height, edge_row, 0, unroll=4)
    for k in range(3):
        lat_out[0, 0, k] = row_of(cells, k).astype(BF)
        lat_out[0, 1, k] = row_of(cells, height - 3 + k).astype(BF)
    hal[...] = jnp.zeros_like(hal)
    ops[lon] = jnp.zeros(ops.shape[1:], BF)
    ops[lon, :channels, :] = hw_ref[0]
    ops[lon, channels : channels + levels, :] = lw_ref[0]
    ops[lon, err_row : err_row + 1, :levels] = err_ref[...]
    sides = lax.min(lat, 1) + lax.min(lats - 1 - lat, 1)
    pl.semaphore_wait(barrier, half + 1 + 3 * sides)
    start_lat(*wires(0))
    start_side(*wires(0))
    mine = ops.at[lon]
    sends = [
        remote(mine, mine, op_send.at[j], op_recv.at[lon], {"lat": lat, "lon": b})
        for j, b in enumerate([partner] + peers)
    ]
    for copy in sends:
        copy.start()
    tap_rows[...] = jnp.zeros_like(tap_rows)
    for row in range(7):
        tap_rows[8 * row : 8 * row + 7, :] = k_ref[row].astype(F32)
    taps[...] = tap_rows[...].T.astype(BF)
    build_rows(taps[...], False, height, breadth, a1)
    pwt[...] = pw_ref[...].astype(F32).T.astype(BF)

    def own_state(p, at):
        return [state[2 * p], state[2 * p + 1]]

    conv_own(own_state, a1, part, height, breadth, channels // 2)
    side_weights(k_ref, False, w1)
    prepare(
        owner, index, weight, obs_t, meta, wt, p_mat, pt_mat, obs_slot, height, breadth
    )
    end_exchange(*wires(0))
    take_rows(lat_in.at[0], hal, channels)
    side_sum(right_in.at[0], left_in.at[0], w1, m_sc, c_sc, ct_sc)

    def add_edge(p, carry):
        for e, got in enumerate(conv_edge(hal, a1, p, height, breadth)):
            at = pl.ds(pl.multiple_of((p * 2 + e) * height, height), height)
            part[at, :] = part[at, :] + got
        return carry

    lax.fori_loop(0, channels // 2, add_edge, 0, unroll=4)

    forwards = []
    for j, b in enumerate(peers):
        copy = remote(
            ops.at[b], ops.at[b], op_send.at[half + j], op_recv.at[b], {"lat": lat, "lon": partner}
        )
        copy.wait_recv()
        copy.start()
        forwards.append(copy)

    build_rows(taps[...], True, height, breadth, a2)
    side_weights(k_ref, True, w2)
    a, c3 = 0.7978845608028654, 0.044715

    def ahead(q, carry):
        r = q * 2
        place = [side_place(r + t, height, breadth) for t in range(2)]
        side = nn(ct_sc[...], jnp.concatenate(place, axis=1))
        mixed = jnp.concatenate([row_of(part, r), row_of(part, r + 1)], axis=1) + side
        pre = nn(pwt[...], mixed.astype(BF))
        square = pre * pre
        t = jnp.tanh(a * (pre + c3 * (square * pre)))
        gate = 0.5 * (1.0 + t)
        slope = gate + (0.5 * pre) * (1.0 - t * t) * (a * (1.0 + (3.0 * c3) * square))
        two = pl.ds(pl.multiple_of(q * 2 * breadth, 2 * breadth), 2 * breadth)
        grid_f[:, two] = slope
        here = jnp.concatenate([row_of(cells, r), row_of(cells, r + 1)], axis=1)
        ana[:, two] = (here + pre * gate).astype(BF)
        return carry

    lax.fori_loop(0, height // 2, ahead, 0, unroll=2)
    total = nt(wt[...], ana[...])
    prof[...] = nn(p_mat[...], total.astype(BF)).astype(BF)

    for j in range(half):
        b = lax.rem(partner + 2 * j, lons)
        remote(
            ops.at[b], ops.at[b], op_send.at[0], op_recv.at[b], {"lat": lat, "lon": partner}
        ).wait_recv()

    def instrument(o, carry):
        at = pl.ds(pl.multiple_of(o * CAP, CAP), CAP)
        hw = ops[o, :channels, :]
        lw = ops[o, channels : channels + levels, :]
        err = ops[o, err_row : err_row + 1, :levels].astype(F32)
        squashed = jnp.tanh(nn(prof[at, :], hw))
        misfit = nt(squashed.astype(BF), lw) - obs_slot[at, :].astype(F32)
        mis[at, :] = misfit.astype(BF)
        back = nn((err * misfit).astype(BF), lw) * (1.0 - squashed * squashed)
        adj[at, :] = nt(back.astype(BF), hw).astype(BF)
        return carry

    lax.fori_loop(0, lons, instrument, 0, unroll=4)
    dep_ref[...] = nn(pt_mat[...], mis[...]).T.astype(BF)
    adj_t = nn(pt_mat[...], adj[...]).T.astype(BF)

    def behind(q, carry):
        r = q * 2
        two = pl.ds(pl.multiple_of(q * 2 * breadth, 2 * breadth), 2 * breadth)
        fb = nn(adj_t, wt[:, two])
        gate = (fb * grid_f[:, two]).astype(BF)
        grid_f[:, two] = fb
        mb = nn(pw_ref[...], gate)
        for t in range(2):
            mine = mb[:, t * breadth : (t + 1) * breadth]
            back[pl.ds(r + t, channels, stride=height), :] = mine
            edge[1, r + t] = nt(pick, mine.astype(BF)).astype(BF)
        return carry

    last = height // 2
    lax.fori_loop(0, 2, behind, 0, unroll=2)
    lax.fori_loop(last - 2, last, behind, 0, unroll=2)
    for k in range(3):
        lat_out[1, 0, k] = row_of(back, k).astype(BF)
        lat_out[1, 1, k] = row_of(back, height - 3 + k).astype(BF)
    start_lat(*wires(1))
    lax.fori_loop(2, last - 2, behind, 0, unroll=2)
    start_side(*wires(1))

    def own_back(p, at):
        both = back[at, :].astype(BF)
        return [both[:height], both[height:]]

    conv_own(own_back, a2, part, height, breadth, channels // 2)
    for copy in sends + forwards:
        copy.wait_send()
    end_exchange(*wires(1))
    take_rows(lat_in.at[1], hal, channels)
    side_sum(right_in.at[1], left_in.at[1], w2, m_sc, c_sc, ct_sc)

    def add_side(q, carry):
        r = q * 2
        two = pl.ds(pl.multiple_of(q * 2 * breadth, 2 * breadth), 2 * breadth)
        place = [side_place(r + t, height, breadth) for t in range(2)]
        side = nn(ct_sc[...], jnp.concatenate(place, axis=1)) + grid_f[:, two]
        for t in range(2):
            cells[pl.ds(r + t, channels, stride=height), :] = side[
                :, t * breadth : (t + 1) * breadth
            ]
        return carry

    lax.fori_loop(0, height // 2, add_side, 0, unroll=2)

    def finish(p, carry):
        for e, got in enumerate(conv_edge(hal, a2, p, height, breadth)):
            c = p * 2 + e
            at = pl.ds(pl.multiple_of(c * height, height), height)
            out_ref[c] = (cells[at, :] + part[at, :] + got).astype(BF)
        return carry

    lax.fori_loop(0, channels // 2, finish, 0, unroll=4)


def body(
    state,
    depth_kernel,
    point_weight,
    column_index,
    column_weight,
    owner,
    observed,
    hidden_weight,
    level_weight,
    inverse_error,
):
    channels, height, breadth = state.shape
    obs, levels = observed.shape
    hid = hidden_weight.shape[2]
    lats, n = lax.axis_size("lat"), lax.axis_size("lon")
    slots = n * CAP
    depth = channels + levels + (-(channels + levels)) % 16 + 16
    args = (
        state,
        hidden_weight,
        level_weight.transpose(0, 2, 1),
        inverse_error,
        owner.T,
        column_index.T,
        column_weight.T,
        observed.T,
        depth_kernel.transpose(1, 2, 0),
        point_weight,
    )
    rows = height + 6
    vm = pltpu.VMEM
    grad, departures = pl.pallas_call(
        lambda *refs: kernel(lats, n, *refs),
        out_shape=(
            jax.ShapeDtypeStruct((channels, height, breadth), BF),
            jax.ShapeDtypeStruct((levels, obs), BF),
        ),
        in_specs=[VM] * len(args),
        out_specs=(VM, VM),
        scratch_shapes=[
            vm((channels * height, breadth), F32),
            vm((channels * height, breadth), F32),
            vm((channels * height, breadth), F32),
            vm((2, channels * height, breadth), F32),
            vm((2, channels * height, breadth), F32),
            vm((21, 8, channels), F32),
            vm((21, 8, channels), F32),
            vm((3, rows, 8, channels), F32),
            vm((8 * height, channels), F32),
            vm((channels, 8 * height), BF),
            vm((channels * 8, breadth), F32),
            vm((2, 2, 3, channels, breadth), BF),
            vm((2, 2, 3, channels, breadth), BF),
            vm((8, obs), F32),
            vm((64, channels), F32),
            vm((channels, 64), BF),
            vm((channels, channels), BF),
            vm((2, height, 8, channels), BF),
            vm((2, rows, 8, channels), BF),
            vm((2, rows, 8, channels), BF),
            vm((n, depth, hid), BF),
            vm((obs, height * breadth), BF),
            vm((slots, obs), BF),
            vm((obs, slots), BF),
            vm((slots, levels), BF),
            vm((channels, height * breadth), F32),
            vm((channels, height * breadth), BF),
            vm((slots, channels), BF),
            vm((slots, channels), BF),
            vm((slots, levels), BF),
            pltpu.SemaphoreType.DMA((2, 8)),
            pltpu.SemaphoreType.DMA((2, 8)),
            pltpu.SemaphoreType.DMA((n,)),
            pltpu.SemaphoreType.DMA((n,)),
        ],
        compiler_params=pltpu.CompilerParams(
            vmem_limit_bytes=56 << 20, collective_id=0, has_side_effects=True
        ),
    )(*args)
    return (grad, departures.T)


def solution(mesh):
    in_specs = (
        P(None, "lat", "lon"),
        P(),
        P(),
        P(("lat", "lon"), None),
        P(("lat", "lon"), None),
        P(("lat", "lon"), None),
        P(("lat", "lon"), None),
        P("lon", None, None),
        P("lon", None, None),
        P("lon", None),
    )
    out_specs = (P(None, "lat", "lon"), P(("lat", "lon"), None))
    return jax.shard_map(body, mesh=mesh, in_specs=in_specs, out_specs=out_specs, check_vma=False)
```

```python
import jax
import jax.numpy as jnp
from jax import lax
from jax.experimental import pallas as pl
from jax.experimental.pallas import tpu as pltpu
from jax.sharding import PartitionSpec as P

CAP = 64
F32 = jnp.float32
BF = jnp.bfloat16
VM = pl.BlockSpec(memory_space=pltpu.VMEM)


def nn(a, b):
    return jnp.dot(a, b, preferred_element_type=F32)


def nt(a, b):
    return lax.dot_general(a, b, (((1,), (1,)), ((), ())), preferred_element_type=F32)


def shifted(v, shift):
    breadth = v.shape[1]
    if not shift:
        return v
    lane = lax.broadcasted_iota(jnp.int32, v.shape, 1)
    keep = lane < breadth - shift if shift > 0 else lane >= -shift
    return jnp.where(keep, pltpu.roll(v, (-shift) % breadth, 1), jnp.zeros_like(v))


def side_weights(k_ref, flip, w_ref):
    channels = k_ref.shape[2]
    slot = lax.broadcasted_iota(jnp.int32, (8, channels), 0)
    for a in range(7):
        taps = k_ref[6 - a if flip else a].astype(F32)
        for d in range(3):
            r, l = (d, 6 - d) if flip else (6 - d, d)
            right = jnp.where(slot >= 5 + d, jnp.broadcast_to(taps[r : r + 1], slot.shape), 0.0)
            left = jnp.where(slot <= 2 - d, jnp.broadcast_to(taps[l : l + 1], slot.shape), 0.0)
            w_ref[a * 3 + d] = right + left


def conv_own(x, out, weights, base):
    height, _, breadth = x.shape
    at = pl.ds(base, 16)
    acc = [None] * height
    for col in range(7):
        w = weights(col)
        part = [None] * height
        for r in range(height):
            v = shifted(x[r, at, :], col - 3)
            for row in range(7):
                i = r + 3 - row
                if 0 <= i < height:
                    term = w[row] * v
                    part[i] = term if part[i] is None else part[i] + term
            for i in range(height):
                if part[i] is not None and r == min(i + 3, height - 1):
                    whole = part[i].astype(F32)
                    acc[i] = whole if acc[i] is None else acc[i] + whole
                    part[i] = None
    for i in range(height):
        out[i, at, :] = acc[i]


def conv_edge(lat_in, out, weights, base):
    height = out.shape[0]
    at = pl.ds(base, 16)
    acc = {}
    for col in range(7):
        w = weights(col)
        part = {}
        for t in range(2):
            for k in range(3):
                v = shifted(lat_in[t, k, at, :], col - 3)
                span = range(0, k + 1) if t == 0 else range(height - 3 + k, height)
                for i in span:
                    term = w[k - i if t == 0 else height + 3 + k - i] * v
                    part[i] = part[i] + term if i in part else term
        for i, v in part.items():
            whole = v.astype(F32)
            acc[i] = acc[i] + whole if i in acc else whole
    for i, v in acc.items():
        out[i, at, :] = out[i, at, :] + v


def side_sum(right_in, left_in, w_ref, m_ref, c_ref, ct_ref):
    rows, _, channels = right_in.shape
    height = rows - 6
    slot = lax.broadcasted_iota(jnp.int32, (8, channels), 0)

    def turn(r, carry):
        both = jnp.where(slot < 4, right_in[r].astype(F32), left_in[r].astype(F32))
        for d in range(3):
            m_ref[d, r] = jnp.where(
                slot >= 5, pltpu.roll(both, 5 + d, 0), pltpu.roll(both, 3 - d, 0)
            )
        return carry

    lax.fori_loop(0, rows, turn, 0, unroll=2)

    def group(g, carry):
        acc = [jnp.zeros((8, channels), F32) for _ in range(4)]
        for d in range(3):
            for a in range(7):
                w = w_ref[a * 3 + d]
                for i in range(4):
                    acc[i] = acc[i] + w * m_ref[d, g * 4 + i + a]
        for i in range(4):
            c_ref[pl.ds(pl.multiple_of((g * 4 + i) * 8, 8), 8), :] = acc[i]
        return carry

    lax.fori_loop(0, height // 4, group, 0)
    ct_ref[...] = c_ref[...].T.astype(BF)


def side_place(i, height, breadth):
    part = lax.broadcasted_iota(jnp.int32, (8 * height, breadth), 0)
    lane = lax.broadcasted_iota(jnp.int32, (8 * height, breadth), 1)
    s = part - i * 8
    hit = ((s >= 0) & (s < 3) & (lane == s)) | ((s > 4) & (s < 8) & (lane == s + breadth - 8))
    return jnp.where(hit, 1.0, 0.0).astype(BF)


def prepare(owner, index, weight, obs_t, meta, wt_ref, p_ref, pt_ref, obs_slot, height, breadth):
    obs = wt_ref.shape[0]
    slots = p_ref.shape[0]
    n = slots // CAP
    si = lax.broadcasted_iota(jnp.int32, (obs, obs), 0)
    sj = lax.broadcasted_iota(jnp.int32, (obs, obs), 1)
    earlier = jnp.where(si < sj, 1.0, 0.0).astype(BF)
    own = owner[...]
    hot = jnp.where(lax.broadcasted_iota(jnp.int32, (n, obs), 0) == own, 1.0, 0.0)
    within = jnp.sum(nn(hot.astype(BF), earlier) * hot, axis=0, keepdims=True)
    slot_row = own * CAP + within.astype(jnp.int32)
    corner = index[0:1, :].astype(F32)
    row0 = jnp.floor((corner + 0.5) / breadth)
    meta[...] = jnp.zeros_like(meta)
    meta[0:4, :] = weight[...].astype(F32)
    meta[4:5, :] = row0
    meta[5:6, :] = corner - row0 * breadth
    meta[6:7, :] = slot_row.astype(F32)
    by_obs = meta[...].T
    w = by_obs[:, 0:4]
    whole = by_obs.astype(jnp.int32)
    lane = lax.broadcasted_iota(jnp.int32, (obs, breadth), 1)
    r0 = jnp.broadcast_to(whole[:, 4:5], (obs, breadth))
    c0 = jnp.broadcast_to(whole[:, 5:6], (obs, breadth))
    zero = jnp.zeros((obs, breadth), F32)
    first = lane == c0
    second = lane == c0 + 1
    top = jnp.where(first, w[:, 0:1], jnp.where(second, w[:, 1:2], zero))
    bottom = jnp.where(first, w[:, 2:3], jnp.where(second, w[:, 3:4], zero))
    for r in range(height):
        wt_ref[:, r * breadth : (r + 1) * breadth] = jnp.where(r0 == r, top, jnp.where(r0 == r - 1, bottom, zero)).astype(BF)
    place = lax.broadcasted_iota(jnp.int32, (slots, obs), 0) == slot_row
    p = jnp.where(place, 1.0, 0.0).astype(BF)
    p_ref[...] = p
    place = lax.broadcasted_iota(jnp.int32, (obs, slots), 1) == whole[:, 6:7]
    pt_ref[...] = jnp.where(place, 1.0, 0.0).astype(BF)
    obs_slot[...] = nt(p, obs_t[...]).astype(BF)


def remote(src, dst, send, recv, device):
    return pltpu.make_async_remote_copy(
        src_ref=src,
        dst_ref=dst,
        send_sem=send,
        recv_sem=recv,
        device_id=device,
        device_id_type=pl.DeviceIdType.MESH,
    )


def selector(breadth):
    s = lax.broadcasted_iota(jnp.int32, (8, breadth), 0)
    lane = lax.broadcasted_iota(jnp.int32, (8, breadth), 1)
    near = (s < 3) & (lane == s)
    far = (s > 4) & (lane == s + (breadth - 8))
    return jnp.where(near | far, 1.0, 0.0).astype(BF)


def copies(grid, lat_in, edge, right_in, left_in, send, recv, lats, lons):
    height = edge.shape[0]
    lat, lon = lax.axis_index("lat"), lax.axis_index("lon")
    left, right = lax.rem(lon + lons - 1, lons), lax.rem(lon + 1, lons)
    low, high, mid = pl.ds(0, 3), pl.ds(height + 3, 3), pl.ds(3, height)
    end = pl.ds(height - 3, 3)

    def make(i, a, b, device):
        return remote(a, b, send.at[i], recv.at[i], device)

    side = [
        make(2, edge, right_in.at[mid], {"lat": lat, "lon": left}),
        make(3, edge, left_in.at[mid], {"lat": lat, "lon": right}),
    ]
    u, d = lax.max(lat - 1, 0), lax.min(lat + 1, lats - 1)
    up = [
        make(0, grid.at[low], lat_in.at[1], {"lat": u, "lon": lon}),
        make(4, edge.at[low], right_in.at[high], {"lat": u, "lon": left}),
        make(5, edge.at[low], left_in.at[high], {"lat": u, "lon": right}),
    ]
    down = [
        make(1, grid.at[end], lat_in.at[0], {"lat": d, "lon": lon}),
        make(6, edge.at[end], right_in.at[low], {"lat": d, "lon": left}),
        make(7, edge.at[end], left_in.at[low], {"lat": d, "lon": right}),
    ]
    return lat > 0, lat < lats - 1, up, down, side


def start_lat(grid, lat_in, edge, right_in, left_in, send, recv, lats, lons):
    height = edge.shape[0]
    has_up, has_down, up, down, side = copies(
        grid, lat_in, edge, right_in, left_in, send, recv, lats, lons
    )

    @pl.when(has_up)
    def _():
        for copy in up:
            copy.start()

    @pl.when(has_down)
    def _():
        for copy in down:
            copy.start()

    for has, t, at in ((has_up, 0, 0), (has_down, 1, height + 3)):

        @pl.when(jnp.logical_not(has))
        def _():
            lat_in[t] = jnp.zeros(lat_in.shape[1:], BF)
            for ref in (right_in, left_in):
                ref[at : at + 3] = jnp.zeros((3,) + ref.shape[1:], BF)


def start_side(*refs):
    for copy in copies(*refs)[4]:
        copy.start()


def end_exchange(*refs):
    has_up, has_down, up, down, side = copies(*refs)

    @pl.when(has_up)
    def _():
        for copy in down:
            copy.wait_recv()
        for copy in up:
            copy.wait_send()

    @pl.when(has_down)
    def _():
        for copy in up:
            copy.wait_recv()
        for copy in down:
            copy.wait_send()

    for copy in side:
        copy.wait()


def kernel(
    lats,
    lons,
    state,
    hw_ref,
    lw_ref,
    err_ref,
    owner,
    index,
    weight,
    obs_t,
    k_ref,
    pw_ref,
    out_ref,
    dep_ref,
    cells,
    x1,
    x2,
    part,
    wide,
    w1,
    w2,
    m_sc,
    c_sc,
    ct_sc,
    lat_in,
    meta,
    tap_rows,
    taps,
    pwt,
    edge,
    right_in,
    left_in,
    ops,
    wt,
    p_mat,
    pt_mat,
    obs_slot,
    grid_f,
    ana,
    prof,
    adj,
    mis,
    send,
    recv,
    op_send,
    op_recv,
):
    channels, height, breadth = state.shape
    levels = obs_t.shape[0]
    err_row = ops.shape[1] - 16
    lat, lon = lax.axis_index("lat"), lax.axis_index("lon")
    partner = lon + 1 - 2 * lax.rem(lon, 2)
    other = lax.rem(lon + lons - 1 + 2 * lax.rem(lon, 2), lons)
    half = lons // 2
    peers = [lax.rem(lon + 2 * j, lons) for j in range(1, half)]
    barrier = pltpu.get_barrier_semaphore()

    def greet(a, b):
        pl.semaphore_signal(
            barrier,
            inc=1,
            device_id={"lat": a, "lon": b},
            device_id_type=pl.DeviceIdType.MESH,
        )

    for b in [partner, other] + peers:
        greet(lat, b)

    @pl.when(lat > 0)
    def _():
        for b in (partner, lon, other):
            greet(lat - 1, b)

    @pl.when(lat < lats - 1)
    def _():
        for b in (partner, lon, other):
            greet(lat + 1, b)

    cells[...] = state[...].reshape(channels * height, breadth).astype(F32)

    grids = (x1, x2)

    def wires(k):
        return (
            grids[k],
            lat_in.at[k],
            edge.at[k],
            right_in.at[k],
            left_in.at[k],
            send.at[k],
            recv.at[k],
            lats,
            lons,
        )

    def row_of(ref, r):
        return ref[pl.ds(r, channels, stride=height), :]

    pick = selector(breadth)

    def edge_row(r, carry):
        mine = row_of(cells, r).astype(BF)
        x1[r] = mine
        edge[0, r] = nt(pick, mine).astype(BF)
        return carry

    lax.fori_loop(0, height, edge_row, 0, unroll=8)
    ops[lon] = jnp.zeros(ops.shape[1:], BF)
    ops[lon, :channels, :] = hw_ref[0]
    ops[lon, channels : channels + levels, :] = lw_ref[0]
    ops[lon, err_row : err_row + 1, :levels] = err_ref[...]
    sides = lax.min(lat, 1) + lax.min(lats - 1 - lat, 1)
    pl.semaphore_wait(barrier, half + 1 + 3 * sides)
    start_lat(*wires(0))
    start_side(*wires(0))
    mine = ops.at[lon]
    sends = [
        remote(mine, mine, op_send.at[j], op_recv.at[lon], {"lat": lat, "lon": b})
        for j, b in enumerate([partner] + peers)
    ]
    for copy in sends:
        copy.start()
    tap_rows[...] = jnp.zeros_like(tap_rows)
    for row in range(7):
        tap_rows[8 * row : 8 * row + 7, :] = k_ref[row].astype(F32)
    taps[...] = tap_rows[...].T
    pwt[...] = pw_ref[...].astype(F32).T.astype(BF)

    def group(g, carry):
        base = pl.multiple_of(g * 16, 16)
        local = taps[pl.ds(base, 16), :]

        def spread(col):
            out = []
            for row in range(7):
                t = row * 8 + col
                w = jnp.broadcast_to(local[:, t : t + 1], (16, breadth)).astype(BF)
                wide[g, row * 7 + col] = w
                out.append(w)
            return out

        conv_own(x1, part, spread, base)
        return carry

    lax.fori_loop(0, channels // 16, group, 0)

    def straight(g):
        return lambda col: [wide[g, row * 7 + col] for row in range(7)]

    def flipped(g):
        return lambda col: [wide[g, (6 - row) * 7 + 6 - col] for row in range(7)]

    side_weights(k_ref, False, w1)
    prepare(
        owner, index, weight, obs_t, meta, wt, p_mat, pt_mat, obs_slot, height, breadth
    )
    end_exchange(*wires(0))
    side_sum(right_in.at[0], left_in.at[0], w1, m_sc, c_sc, ct_sc)

    def add_edge(g, carry):
        conv_edge(lat_in.at[0], part, straight(g), pl.multiple_of(g * 16, 16))
        return carry

    lax.fori_loop(0, channels // 16, add_edge, 0, unroll=2)

    forwards = []
    for j, b in enumerate(peers):
        copy = remote(
            ops.at[b], ops.at[b], op_send.at[half + j], op_recv.at[b], {"lat": lat, "lon": partner}
        )
        copy.wait_recv()
        copy.start()
        forwards.append(copy)

    side_weights(k_ref, True, w2)
    a, c3 = 0.7978845608028654, 0.044715

    def ahead(q, carry):
        r = q * 2
        place = [side_place(r + t, height, breadth) for t in range(2)]
        side = nn(ct_sc[...], jnp.concatenate(place, axis=1))
        mixed = jnp.concatenate([part[r], part[r + 1]], axis=1) + side
        pre = nn(pwt[...], mixed.astype(BF))
        square = pre * pre
        t = jnp.tanh(a * (pre + c3 * (square * pre)))
        gate = 0.5 * (1.0 + t)
        slope = gate + (0.5 * pre) * (1.0 - t * t) * (a * (1.0 + (3.0 * c3) * square))
        two = pl.ds(pl.multiple_of(q * 2 * breadth, 2 * breadth), 2 * breadth)
        grid_f[:, two] = slope
        here = jnp.concatenate([x1[r], x1[r + 1]], axis=1).astype(F32)
        ana[:, two] = (here + pre * gate).astype(BF)
        return carry

    lax.fori_loop(0, height // 2, ahead, 0, unroll=2)
    total = nt(wt[...], ana[...])
    prof[...] = nn(p_mat[...], total.astype(BF)).astype(BF)

    for j in range(half):
        b = lax.rem(partner + 2 * j, lons)
        remote(
            ops.at[b], ops.at[b], op_send.at[0], op_recv.at[b], {"lat": lat, "lon": partner}
        ).wait_recv()

    def instrument(o, carry):
        at = pl.ds(pl.multiple_of(o * CAP, CAP), CAP)
        hw = ops[o, :channels, :]
        lw = ops[o, channels : channels + levels, :]
        err = ops[o, err_row : err_row + 1, :levels].astype(F32)
        squashed = jnp.tanh(nn(prof[at, :], hw))
        misfit = nt(squashed.astype(BF), lw) - obs_slot[at, :].astype(F32)
        mis[at, :] = misfit.astype(BF)
        back = nn((err * misfit).astype(BF), lw) * (1.0 - squashed * squashed)
        adj[at, :] = nt(back.astype(BF), hw).astype(BF)
        return carry

    lax.fori_loop(0, lons, instrument, 0, unroll=4)
    dep_ref[...] = nn(pt_mat[...], mis[...]).T.astype(BF)
    adj_t = nn(pt_mat[...], adj[...]).T.astype(BF)

    def behind(q, carry):
        r = q * 2
        two = pl.ds(pl.multiple_of(q * 2 * breadth, 2 * breadth), 2 * breadth)
        fb = nn(adj_t, wt[:, two])
        gate = (fb * grid_f[:, two]).astype(BF)
        grid_f[:, two] = fb
        mb = nn(pw_ref[...], gate).astype(BF)
        for t in range(2):
            mine = mb[:, t * breadth : (t + 1) * breadth]
            x2[r + t] = mine
            edge[1, r + t] = nt(pick, mine).astype(BF)
        return carry

    last = height // 2
    lax.fori_loop(0, 2, behind, 0, unroll=2)
    lax.fori_loop(last - 2, last, behind, 0, unroll=2)
    start_lat(*wires(1))
    lax.fori_loop(2, last - 2, behind, 0, unroll=2)
    start_side(*wires(1))

    def group_back(g, carry):
        conv_own(x2, part, flipped(g), pl.multiple_of(g * 16, 16))
        return carry

    lax.fori_loop(0, channels // 16, group_back, 0)
    for copy in sends + forwards:
        copy.wait_send()
    end_exchange(*wires(1))
    side_sum(right_in.at[1], left_in.at[1], w2, m_sc, c_sc, ct_sc)

    def edge_back(g, carry):
        conv_edge(lat_in.at[1], part, flipped(g), pl.multiple_of(g * 16, 16))
        return carry

    lax.fori_loop(0, channels // 16, edge_back, 0, unroll=2)

    def add_side(q, carry):
        r = q * 2
        two = pl.ds(pl.multiple_of(q * 2 * breadth, 2 * breadth), 2 * breadth)
        place = [side_place(r + t, height, breadth) for t in range(2)]
        side = nn(ct_sc[...], jnp.concatenate(place, axis=1)) + grid_f[:, two]
        for t in range(2):
            cells[pl.ds(r + t, channels, stride=height), :] = (
                side[:, t * breadth : (t + 1) * breadth] + part[r + t]
            )
        return carry

    lax.fori_loop(0, height // 2, add_side, 0, unroll=2)
    out_ref[...] = cells[...].astype(BF).reshape(out_ref.shape)


def body(
    state,
    depth_kernel,
    point_weight,
    column_index,
    column_weight,
    owner,
    observed,
    hidden_weight,
    level_weight,
    inverse_error,
):
    channels, height, breadth = state.shape
    obs, levels = observed.shape
    hid = hidden_weight.shape[2]
    lats, n = lax.axis_size("lat"), lax.axis_size("lon")
    slots = n * CAP
    depth = channels + levels + (-(channels + levels)) % 16 + 16
    args = (
        state,
        hidden_weight,
        level_weight.transpose(0, 2, 1),
        inverse_error,
        owner.T,
        column_index.T,
        column_weight.T,
        observed.T,
        depth_kernel.transpose(1, 2, 0),
        point_weight,
    )
    rows = height + 6
    vm = pltpu.VMEM
    grad, departures = pl.pallas_call(
        lambda *refs: kernel(lats, n, *refs),
        out_shape=(
            jax.ShapeDtypeStruct((channels, height, breadth), BF),
            jax.ShapeDtypeStruct((levels, obs), BF),
        ),
        in_specs=[VM] * len(args),
        out_specs=(VM, VM),
        scratch_shapes=[
            vm((channels * height, breadth), F32),
            vm((height, channels, breadth), BF),
            vm((height, channels, breadth), BF),
            vm((height, channels, breadth), F32),
            vm((channels // 16, 49, 16, breadth), BF),
            vm((21, 8, channels), F32),
            vm((21, 8, channels), F32),
            vm((3, rows, 8, channels), F32),
            vm((8 * height, channels), F32),
            vm((channels, 8 * height), BF),
            vm((2, 2, 3, channels, breadth), BF),
            vm((8, obs), F32),
            vm((64, channels), F32),
            vm((channels, 64), F32),
            vm((channels, channels), BF),
            vm((2, height, 8, channels), BF),
            vm((2, rows, 8, channels), BF),
            vm((2, rows, 8, channels), BF),
            vm((n, depth, hid), BF),
            vm((obs, height * breadth), BF),
            vm((slots, obs), BF),
            vm((obs, slots), BF),
            vm((slots, levels), BF),
            vm((channels, height * breadth), F32),
            vm((channels, height * breadth), BF),
            vm((slots, channels), BF),
            vm((slots, channels), BF),
            vm((slots, levels), BF),
            pltpu.SemaphoreType.DMA((2, 8)),
            pltpu.SemaphoreType.DMA((2, 8)),
            pltpu.SemaphoreType.DMA((n,)),
            pltpu.SemaphoreType.DMA((n,)),
        ],
        compiler_params=pltpu.CompilerParams(
            vmem_limit_bytes=56 << 20, collective_id=0, has_side_effects=True
        ),
    )(*args)
    return (grad, departures.T)


def solution(mesh):
    in_specs = (
        P(None, "lat", "lon"),
        P(),
        P(),
        P(("lat", "lon"), None),
        P(("lat", "lon"), None),
        P(("lat", "lon"), None),
        P(("lat", "lon"), None),
        P("lon", None, None),
        P("lon", None, None),
        P("lon", None),
    )
    out_specs = (P(None, "lat", "lon"), P(("lat", "lon"), None))
    return jax.shard_map(body, mesh=mesh, in_specs=in_specs, out_specs=out_specs, check_vma=False)
```

```python
import jax
import jax.numpy as jnp
from jax import lax
from jax.experimental import pallas as pl
from jax.experimental.pallas import tpu as pltpu
from jax.sharding import PartitionSpec as P

CAP = 64
F32 = jnp.float32
BF = jnp.bfloat16
VM = pl.BlockSpec(memory_space=pltpu.VMEM)


def nn(a, b):
    return jnp.dot(a, b, preferred_element_type=F32)


def nt(a, b):
    return lax.dot_general(a, b, (((1,), (1,)), ((), ())), preferred_element_type=F32)


def flip_bit(q, bit):
    return q + bit * (1 - 2 * lax.rem(lax.div(q, bit), 2))


def shifted(v, shift):
    breadth = v.shape[1]
    if not shift:
        return v
    lane = lax.broadcasted_iota(jnp.int32, v.shape, 1)
    keep = lane < breadth - shift if shift > 0 else lane >= -shift
    return jnp.where(keep, pltpu.roll(v, (-shift) % breadth, 1), jnp.zeros_like(v))


def side_weights(k_ref, flip, w_ref):
    channels = k_ref.shape[2]
    slot = lax.broadcasted_iota(jnp.int32, (8, channels), 0)
    for a in range(7):
        taps = k_ref[6 - a if flip else a].astype(F32)
        for d in range(3):
            r, l = (d, 6 - d) if flip else (6 - d, d)
            right = jnp.where(slot >= 5 + d, jnp.broadcast_to(taps[r : r + 1], slot.shape), 0.0)
            left = jnp.where(slot <= 2 - d, jnp.broadcast_to(taps[l : l + 1], slot.shape), 0.0)
            w_ref[a * 3 + d] = right + left


def conv_own(x, out, weights, base):
    height, _, breadth = x.shape
    at = pl.ds(base, 16)
    acc = [None] * height
    for col in range(7):
        w = weights(col)
        part = [None] * height
        for r in range(height):
            v = shifted(x[r, at, :], col - 3)
            for row in range(7):
                i = r + 3 - row
                if 0 <= i < height:
                    term = w[row] * v
                    part[i] = term if part[i] is None else part[i] + term
            for i in range(height):
                if part[i] is not None and r == min(i + 3, height - 1):
                    whole = part[i].astype(F32)
                    acc[i] = whole if acc[i] is None else acc[i] + whole
                    part[i] = None
    for i in range(height):
        out[i, at, :] = acc[i]


def conv_edge(lat_in, out, weights, base):
    height = out.shape[0]
    at = pl.ds(base, 16)
    acc = {}
    for col in range(7):
        w = weights(col)
        part = {}
        for t in range(2):
            for k in range(3):
                v = shifted(lat_in[t, k, at, :], col - 3)
                span = range(0, k + 1) if t == 0 else range(height - 3 + k, height)
                for i in span:
                    term = w[k - i if t == 0 else height + 3 + k - i] * v
                    part[i] = part[i] + term if i in part else term
        for i, v in part.items():
            whole = v.astype(F32)
            acc[i] = acc[i] + whole if i in acc else whole
    for i, v in acc.items():
        out[i, at, :] = out[i, at, :] + v


def side_sum(right_in, left_in, w_ref, m_ref, c_ref, ct_ref):
    rows, _, channels = right_in.shape
    height = rows - 6
    slot = lax.broadcasted_iota(jnp.int32, (8, channels), 0)

    def turn(r, carry):
        both = jnp.where(slot < 4, right_in[r].astype(F32), left_in[r].astype(F32))
        for d in range(3):
            m_ref[d, r] = jnp.where(
                slot >= 5, pltpu.roll(both, 5 + d, 0), pltpu.roll(both, 3 - d, 0)
            )
        return carry

    lax.fori_loop(0, rows, turn, 0, unroll=2)

    def group(g, carry):
        acc = [jnp.zeros((8, channels), F32) for _ in range(4)]
        for d in range(3):
            for a in range(7):
                w = w_ref[a * 3 + d]
                for i in range(4):
                    acc[i] = acc[i] + w * m_ref[d, g * 4 + i + a]
        for i in range(4):
            c_ref[pl.ds(pl.multiple_of((g * 4 + i) * 8, 8), 8), :] = acc[i]
        return carry

    lax.fori_loop(0, height // 4, group, 0)
    ct_ref[...] = c_ref[...].T.astype(BF)


def side_place(i, height, breadth):
    part = lax.broadcasted_iota(jnp.int32, (8 * height, breadth), 0)
    lane = lax.broadcasted_iota(jnp.int32, (8 * height, breadth), 1)
    s = part - i * 8
    hit = ((s >= 0) & (s < 3) & (lane == s)) | ((s > 4) & (s < 8) & (lane == s + breadth - 8))
    return jnp.where(hit, 1.0, 0.0).astype(BF)


def prepare(owner, index, weight, obs_t, meta, wt_ref, p_ref, pt_ref, obs_slot, height, breadth):
    obs = wt_ref.shape[0]
    slots = p_ref.shape[0]
    n = slots // CAP
    si = lax.broadcasted_iota(jnp.int32, (obs, obs), 0)
    sj = lax.broadcasted_iota(jnp.int32, (obs, obs), 1)
    earlier = jnp.where(si < sj, 1.0, 0.0).astype(BF)
    own = owner[...]
    hot = jnp.where(lax.broadcasted_iota(jnp.int32, (n, obs), 0) == own, 1.0, 0.0)
    within = jnp.sum(nn(hot.astype(BF), earlier) * hot, axis=0, keepdims=True)
    slot_row = own * CAP + within.astype(jnp.int32)
    corner = index[0:1, :].astype(F32)
    row0 = jnp.floor((corner + 0.5) / breadth)
    meta[...] = jnp.zeros_like(meta)
    meta[0:4, :] = weight[...].astype(F32)
    meta[4:5, :] = row0
    meta[5:6, :] = corner - row0 * breadth
    meta[6:7, :] = slot_row.astype(F32)
    by_obs = meta[...].T
    w = by_obs[:, 0:4]
    whole = by_obs.astype(jnp.int32)
    lane = lax.broadcasted_iota(jnp.int32, (obs, breadth), 1)
    r0 = jnp.broadcast_to(whole[:, 4:5], (obs, breadth))
    c0 = jnp.broadcast_to(whole[:, 5:6], (obs, breadth))
    zero = jnp.zeros((obs, breadth), F32)
    first = lane == c0
    second = lane == c0 + 1
    top = jnp.where(first, w[:, 0:1], jnp.where(second, w[:, 1:2], zero))
    bottom = jnp.where(first, w[:, 2:3], jnp.where(second, w[:, 3:4], zero))
    for r in range(height):
        wt_ref[:, r * breadth : (r + 1) * breadth] = jnp.where(r0 == r, top, jnp.where(r0 == r - 1, bottom, zero)).astype(BF)
    place = lax.broadcasted_iota(jnp.int32, (slots, obs), 0) == slot_row
    p = jnp.where(place, 1.0, 0.0).astype(BF)
    p_ref[...] = p
    place = lax.broadcasted_iota(jnp.int32, (obs, slots), 1) == whole[:, 6:7]
    pt_ref[...] = jnp.where(place, 1.0, 0.0).astype(BF)
    obs_slot[...] = nt(p, obs_t[...]).astype(BF)


def remote(src, dst, send, recv, device):
    return pltpu.make_async_remote_copy(
        src_ref=src,
        dst_ref=dst,
        send_sem=send,
        recv_sem=recv,
        device_id=device,
        device_id_type=pl.DeviceIdType.MESH,
    )


def selector(breadth):
    s = lax.broadcasted_iota(jnp.int32, (8, breadth), 0)
    lane = lax.broadcasted_iota(jnp.int32, (8, breadth), 1)
    near = (s < 3) & (lane == s)
    far = (s > 4) & (lane == s + (breadth - 8))
    return jnp.where(near | far, 1.0, 0.0).astype(BF)


def copies(grid, lat_in, edge, right_in, left_in, send, recv, lats, lons):
    height = edge.shape[0]
    lat, lon = lax.axis_index("lat"), lax.axis_index("lon")
    left, right = lax.rem(lon + lons - 1, lons), lax.rem(lon + 1, lons)
    low, high, mid = pl.ds(0, 3), pl.ds(height + 3, 3), pl.ds(3, height)
    end = pl.ds(height - 3, 3)

    def make(i, a, b, device):
        return remote(a, b, send.at[i], recv.at[i], device)

    side = [
        make(2, edge, right_in.at[mid], {"lat": lat, "lon": left}),
        make(3, edge, left_in.at[mid], {"lat": lat, "lon": right}),
    ]
    u, d = lax.max(lat - 1, 0), lax.min(lat + 1, lats - 1)
    up = [
        make(0, grid.at[low], lat_in.at[1], {"lat": u, "lon": lon}),
        make(4, edge.at[low], right_in.at[high], {"lat": u, "lon": left}),
        make(5, edge.at[low], left_in.at[high], {"lat": u, "lon": right}),
    ]
    down = [
        make(1, grid.at[end], lat_in.at[0], {"lat": d, "lon": lon}),
        make(6, edge.at[end], right_in.at[low], {"lat": d, "lon": left}),
        make(7, edge.at[end], left_in.at[low], {"lat": d, "lon": right}),
    ]
    return lat > 0, lat < lats - 1, up, down, side


def start_lat(grid, lat_in, edge, right_in, left_in, send, recv, lats, lons):
    height = edge.shape[0]
    has_up, has_down, up, down, side = copies(
        grid, lat_in, edge, right_in, left_in, send, recv, lats, lons
    )

    @pl.when(has_up)
    def _():
        for copy in up:
            copy.start()

    @pl.when(has_down)
    def _():
        for copy in down:
            copy.start()

    for has, t, at in ((has_up, 0, 0), (has_down, 1, height + 3)):

        @pl.when(jnp.logical_not(has))
        def _():
            lat_in[t] = jnp.zeros(lat_in.shape[1:], BF)
            for ref in (right_in, left_in):
                ref[at : at + 3] = jnp.zeros((3,) + ref.shape[1:], BF)


def start_side(*refs):
    for copy in copies(*refs)[4]:
        copy.start()


def end_exchange(*refs):
    has_up, has_down, up, down, side = copies(*refs)

    @pl.when(has_up)
    def _():
        for copy in down:
            copy.wait_recv()
        for copy in up:
            copy.wait_send()

    @pl.when(has_down)
    def _():
        for copy in up:
            copy.wait_recv()
        for copy in down:
            copy.wait_send()

    for copy in side:
        copy.wait()


def kernel(
    lats,
    lons,
    state,
    hw_ref,
    lw_ref,
    err_ref,
    owner,
    index,
    weight,
    obs_t,
    k_ref,
    pw_ref,
    out_ref,
    dep_ref,
    cells,
    x1,
    x2,
    part,
    wide,
    w1,
    w2,
    m_sc,
    c_sc,
    ct_sc,
    lat_in,
    meta,
    tap_rows,
    taps,
    pwt,
    edge,
    right_in,
    left_in,
    ops,
    wt,
    p_mat,
    pt_mat,
    obs_slot,
    grid_f,
    ana,
    prof,
    adj,
    mis,
    send,
    recv,
    op_send,
    op_recv,
):
    channels, height, breadth = state.shape
    levels = obs_t.shape[0]
    err_row = channels + levels
    lat, lon = lax.axis_index("lat"), lax.axis_index("lon")
    partner = lon + 1 - 2 * lax.rem(lon, 2)
    other = lax.rem(lon + lons - 1 + 2 * lax.rem(lon, 2), lons)
    half = lons // 2
    bits = half.bit_length() - 1
    core, chip = lax.rem(lon, 2), lax.div(lon, 2)

    def across(q, t, c):
        first, second = flip_bit(q, 1 << t), flip_bit(q, 1 << (bits - 1 - t))
        return first + c * (second - first)

    def holder(mask, c):
        q = chip
        for t in range(bits):
            if mask >> t & 1:
                q = across(q, t, c)
        return 2 * q + c

    peers = [holder(1 << t, core) for t in range(bits)]
    barrier = pltpu.get_barrier_semaphore()

    def greet(a, b):
        pl.semaphore_signal(
            barrier,
            inc=1,
            device_id={"lat": a, "lon": b},
            device_id_type=pl.DeviceIdType.MESH,
        )

    for b in [partner, other] + peers:
        greet(lat, b)

    @pl.when(lat > 0)
    def _():
        for b in (partner, lon, other):
            greet(lat - 1, b)

    @pl.when(lat < lats - 1)
    def _():
        for b in (partner, lon, other):
            greet(lat + 1, b)

    cells[...] = state[...].reshape(channels * height, breadth).astype(F32)

    grids = (x1, x2)

    def wires(k):
        return (
            grids[k],
            lat_in.at[k],
            edge.at[k],
            right_in.at[k],
            left_in.at[k],
            send.at[k],
            recv.at[k],
            lats,
            lons,
        )

    def row_of(ref, r):
        return ref[pl.ds(r, channels, stride=height), :]

    pick = selector(breadth)

    def edge_row(r, carry):
        mine = row_of(cells, r).astype(BF)
        x1[r] = mine
        edge[0, r] = nt(pick, mine).astype(BF)
        return carry

    lax.fori_loop(0, height, edge_row, 0, unroll=8)
    ops[lon] = jnp.zeros(ops.shape[1:], BF)
    ops[lon, :channels, :] = hw_ref[0]
    ops[lon, channels : channels + levels, :] = lw_ref[0]
    ops[lon, err_row : err_row + 1, :levels] = err_ref[...]
    sides = lax.min(lat, 1) + lax.min(lats - 1 - lat, 1)
    pl.semaphore_wait(barrier, bits + 2 + 3 * sides)
    start_lat(*wires(0))
    start_side(*wires(0))
    started = []

    def op_copy(o, b):
        return remote(
            ops.at[o], ops.at[o], op_send.at[len(started)], op_recv.at[o], {"lat": lat, "lon": b}
        )

    def pass_on(mask):
        o = holder(mask, core)
        if mask:
            op_copy(o, partner).wait_recv()
        for t in range(mask.bit_length(), bits):
            started.append(op_copy(o, peers[t]))
            started[-1].start()
        started.append(op_copy(o, partner))
        started[-1].start()

    pass_on(0)
    tap_rows[...] = jnp.zeros_like(tap_rows)
    for row in range(7):
        tap_rows[8 * row : 8 * row + 7, :] = k_ref[row].astype(F32)
    taps[...] = tap_rows[...].T
    pwt[...] = pw_ref[...].astype(F32).T.astype(BF)

    def group(g, carry):
        base = pl.multiple_of(g * 16, 16)
        local = taps[pl.ds(base, 16), :]

        def spread(col):
            out = []
            for row in range(7):
                t = row * 8 + col
                w = jnp.broadcast_to(local[:, t : t + 1], (16, breadth)).astype(BF)
                wide[g, row * 7 + col] = w
                out.append(w)
            return out

        conv_own(x1, part, spread, base)
        return carry

    lax.fori_loop(0, channels // 16, group, 0)

    def straight(g):
        return lambda col: [wide[g, row * 7 + col] for row in range(7)]

    def flipped(g):
        return lambda col: [wide[g, (6 - row) * 7 + 6 - col] for row in range(7)]

    side_weights(k_ref, False, w1)
    prepare(
        owner, index, weight, obs_t, meta, wt, p_mat, pt_mat, obs_slot, height, breadth
    )
    end_exchange(*wires(0))
    side_sum(right_in.at[0], left_in.at[0], w1, m_sc, c_sc, ct_sc)

    def add_edge(g, carry):
        conv_edge(lat_in.at[0], part, straight(g), pl.multiple_of(g * 16, 16))
        return carry

    lax.fori_loop(0, channels // 16, add_edge, 0, unroll=2)

    side_weights(k_ref, True, w2)
    a, c3 = 0.7978845608028654, 0.044715

    def ahead(q, carry):
        r = q * 2
        place = [side_place(r + t, height, breadth) for t in range(2)]
        side = nn(ct_sc[...], jnp.concatenate(place, axis=1))
        mixed = jnp.concatenate([part[r], part[r + 1]], axis=1) + side
        pre = nn(pwt[...], mixed.astype(BF))
        square = pre * pre
        t = jnp.tanh(a * (pre + c3 * (square * pre)))
        gate = 0.5 * (1.0 + t)
        slope = gate + (0.5 * pre) * (1.0 - t * t) * (a * (1.0 + (3.0 * c3) * square))
        two = pl.ds(pl.multiple_of(q * 2 * breadth, 2 * breadth), 2 * breadth)
        grid_f[:, two] = slope
        here = jnp.concatenate([x1[r], x1[r + 1]], axis=1).astype(F32)
        ana[:, two] = (here + pre * gate).astype(BF)
        return carry

    lax.fori_loop(0, height // 2, ahead, 0, unroll=2)
    pass_on(1)
    total = nt(wt[...], ana[...])
    prof[...] = nn(p_mat[...], total.astype(BF)).astype(BF)

    def instrument(o):
        at = pl.ds(pl.multiple_of(o * CAP, CAP), CAP)
        hw = ops[o, :channels, :]
        lw = ops[o, channels : channels + levels, :]
        err = ops[o, err_row : err_row + 1, :levels].astype(F32)
        squashed = jnp.tanh(nn(prof[at, :], hw))
        misfit = nt(squashed.astype(BF), lw) - obs_slot[at, :].astype(F32)
        mis[at, :] = misfit.astype(BF)
        back = nn((err * misfit).astype(BF), lw) * (1.0 - squashed * squashed)
        adj[at, :] = nt(back.astype(BF), hw).astype(BF)

    def from_partner(mask):
        o = holder(mask, 1 - core)
        op_copy(o, partner).wait_recv()
        return o

    for mask in range(2, half - 1):
        pass_on(mask)
    early = [lon, from_partner(0)] + [holder(mask, core) for mask in range(1, half - 1)]
    for o in early:
        instrument(o)
    if half > 2:
        pass_on(half - 1)
    late = [from_partner(mask) for mask in range(1, half)]
    for o in [holder(half - 1, core)] + late:
        instrument(o)
    dep_ref[...] = nn(pt_mat[...], mis[...]).T.astype(BF)
    adj_t = nn(pt_mat[...], adj[...]).T.astype(BF)

    def behind(q, carry):
        r = q * 2
        two = pl.ds(pl.multiple_of(q * 2 * breadth, 2 * breadth), 2 * breadth)
        fb = nn(adj_t, wt[:, two])
        gate = (fb * grid_f[:, two]).astype(BF)
        grid_f[:, two] = fb
        mb = nn(pw_ref[...], gate).astype(BF)
        for t in range(2):
            mine = mb[:, t * breadth : (t + 1) * breadth]
            x2[r + t] = mine
            edge[1, r + t] = nt(pick, mine).astype(BF)
        return carry

    last = height // 2
    lax.fori_loop(0, 2, behind, 0, unroll=2)
    lax.fori_loop(last - 2, last, behind, 0, unroll=2)
    start_lat(*wires(1))
    lax.fori_loop(2, last - 2, behind, 0, unroll=2)
    start_side(*wires(1))

    def group_back(g, carry):
        conv_own(x2, part, flipped(g), pl.multiple_of(g * 16, 16))
        return carry

    lax.fori_loop(0, channels // 16, group_back, 0)
    for copy in started:
        copy.wait_send()
    end_exchange(*wires(1))
    side_sum(right_in.at[1], left_in.at[1], w2, m_sc, c_sc, ct_sc)

    def edge_back(g, carry):
        conv_edge(lat_in.at[1], part, flipped(g), pl.multiple_of(g * 16, 16))
        return carry

    lax.fori_loop(0, channels // 16, edge_back, 0, unroll=2)

    def add_side(q, carry):
        r = q * 2
        two = pl.ds(pl.multiple_of(q * 2 * breadth, 2 * breadth), 2 * breadth)
        place = [side_place(r + t, height, breadth) for t in range(2)]
        side = nn(ct_sc[...], jnp.concatenate(place, axis=1)) + grid_f[:, two]
        for t in range(2):
            cells[pl.ds(r + t, channels, stride=height), :] = (
                side[:, t * breadth : (t + 1) * breadth] + part[r + t]
            )
        return carry

    lax.fori_loop(0, height // 2, add_side, 0, unroll=2)
    out_ref[...] = cells[...].astype(BF).reshape(out_ref.shape)


def body(
    state,
    depth_kernel,
    point_weight,
    column_index,
    column_weight,
    owner,
    observed,
    hidden_weight,
    level_weight,
    inverse_error,
):
    channels, height, breadth = state.shape
    obs, levels = observed.shape
    hid = hidden_weight.shape[2]
    lats, n = lax.axis_size("lat"), lax.axis_size("lon")
    slots = n * CAP
    depth = channels + levels + 1 + (-(channels + levels + 1)) % 16
    args = (
        state,
        hidden_weight,
        level_weight.transpose(0, 2, 1),
        inverse_error,
        owner.T,
        column_index.T,
        column_weight.T,
        observed.T,
        depth_kernel.transpose(1, 2, 0),
        point_weight,
    )
    rows = height + 6
    vm = pltpu.VMEM
    grad, departures = pl.pallas_call(
        lambda *refs: kernel(lats, n, *refs),
        out_shape=(
            jax.ShapeDtypeStruct((channels, height, breadth), BF),
            jax.ShapeDtypeStruct((levels, obs), BF),
        ),
        in_specs=[VM] * len(args),
        out_specs=(VM, VM),
        scratch_shapes=[
            vm((channels * height, breadth), F32),
            vm((height, channels, breadth), BF),
            vm((height, channels, breadth), BF),
            vm((height, channels, breadth), F32),
            vm((channels // 16, 49, 16, breadth), BF),
            vm((21, 8, channels), F32),
            vm((21, 8, channels), F32),
            vm((3, rows, 8, channels), F32),
            vm((8 * height, channels), F32),
            vm((channels, 8 * height), BF),
            vm((2, 2, 3, channels, breadth), BF),
            vm((8, obs), F32),
            vm((64, channels), F32),
            vm((channels, 64), F32),
            vm((channels, channels), BF),
            vm((2, height, 8, channels), BF),
            vm((2, rows, 8, channels), BF),
            vm((2, rows, 8, channels), BF),
            vm((n, depth, hid), BF),
            vm((obs, height * breadth), BF),
            vm((slots, obs), BF),
            vm((obs, slots), BF),
            vm((slots, levels), BF),
            vm((channels, height * breadth), F32),
            vm((channels, height * breadth), BF),
            vm((slots, channels), BF),
            vm((slots, channels), BF),
            vm((slots, levels), BF),
            pltpu.SemaphoreType.DMA((2, 8)),
            pltpu.SemaphoreType.DMA((2, 8)),
            pltpu.SemaphoreType.DMA((n,)),
            pltpu.SemaphoreType.DMA((n,)),
        ],
        compiler_params=pltpu.CompilerParams(
            vmem_limit_bytes=56 << 20, collective_id=0, has_side_effects=True
        ),
    )(*args)
    return (grad, departures.T)


def solution(mesh):
    in_specs = (
        P(None, "lat", "lon"),
        P(),
        P(),
        P(("lat", "lon"), None),
        P(("lat", "lon"), None),
        P(("lat", "lon"), None),
        P(("lat", "lon"), None),
        P("lon", None, None),
        P("lon", None, None),
        P("lon", None),
    )
    out_specs = (P(None, "lat", "lon"), P(("lat", "lon"), None))
    return jax.shard_map(body, mesh=mesh, in_specs=in_specs, out_specs=out_specs, check_vma=False)
```

```python
import jax
import jax.numpy as jnp
from jax import lax
from jax.experimental import pallas as pl
from jax.experimental.pallas import tpu as pltpu
from jax.sharding import PartitionSpec as P

CAP = 64
F32 = jnp.float32
BF = jnp.bfloat16
VM = pl.BlockSpec(memory_space=pltpu.VMEM)


def nn(a, b):
    return jnp.dot(a, b, preferred_element_type=F32)


def nt(a, b):
    return lax.dot_general(a, b, (((1,), (1,)), ((), ())), preferred_element_type=F32)


def flip_bit(q, bit):
    return q + bit * (1 - 2 * lax.rem(lax.div(q, bit), 2))


def shifted(v, shift):
    breadth = v.shape[1]
    if not shift:
        return v
    lane = lax.broadcasted_iota(jnp.int32, v.shape, 1)
    keep = lane < breadth - shift if shift > 0 else lane >= -shift
    return jnp.where(keep, pltpu.roll(v, (-shift) % breadth, 1), jnp.zeros_like(v))


def side_weights(k_ref, flip, w_ref):
    channels = k_ref.shape[2]
    slot = lax.broadcasted_iota(jnp.int32, (8, channels), 0)
    for a in range(7):
        taps = k_ref[6 - a if flip else a].astype(F32)
        for d in range(3):
            r, l = (d, 6 - d) if flip else (6 - d, d)
            right = jnp.where(slot >= 5 + d, jnp.broadcast_to(taps[r : r + 1], slot.shape), 0.0)
            left = jnp.where(slot <= 2 - d, jnp.broadcast_to(taps[l : l + 1], slot.shape), 0.0)
            w_ref[a * 3 + d] = right + left


def conv_own(x, out, weights, base):
    height, _, breadth = x.shape
    at = pl.ds(base, 16)
    acc = [None] * height
    for col in range(7):
        w = weights(col)
        part = [None] * height
        for r in range(height):
            v = shifted(x[r, at, :], col - 3)
            for row in range(7):
                i = r + 3 - row
                if 0 <= i < height:
                    term = w[row] * v
                    part[i] = term if part[i] is None else part[i] + term
            for i in range(height):
                if part[i] is not None and r == min(i + 3, height - 1):
                    whole = part[i].astype(F32)
                    acc[i] = whole if acc[i] is None else acc[i] + whole
                    part[i] = None
    for i in range(height):
        out[i, at, :] = acc[i]


def conv_edge(lat_in, out, weights, base):
    height = out.shape[0]
    at = pl.ds(base, 16)
    acc = {}
    for col in range(7):
        w = weights(col)
        part = {}
        for t in range(2):
            for k in range(3):
                v = shifted(lat_in[t, k, at, :], col - 3)
                span = range(0, k + 1) if t == 0 else range(height - 3 + k, height)
                for i in span:
                    term = w[k - i if t == 0 else height + 3 + k - i] * v
                    part[i] = part[i] + term if i in part else term
        for i, v in part.items():
            whole = v.astype(F32)
            acc[i] = acc[i] + whole if i in acc else whole
    for i, v in acc.items():
        out[i, at, :] = out[i, at, :] + v


def side_sum(right_in, left_in, w_ref, m_ref, c_ref, ct_ref):
    rows, _, channels = right_in.shape
    height = rows - 6
    slot = lax.broadcasted_iota(jnp.int32, (8, channels), 0)

    def turn(r, carry):
        both = jnp.where(slot < 4, right_in[r].astype(F32), left_in[r].astype(F32))
        for d in range(3):
            m_ref[d, r] = jnp.where(
                slot >= 5, pltpu.roll(both, 5 + d, 0), pltpu.roll(both, 3 - d, 0)
            )
        return carry

    lax.fori_loop(0, rows, turn, 0, unroll=2)

    def group(g, carry):
        acc = [jnp.zeros((8, channels), F32) for _ in range(4)]
        for d in range(3):
            for a in range(7):
                w = w_ref[a * 3 + d]
                for i in range(4):
                    acc[i] = acc[i] + w * m_ref[d, g * 4 + i + a]
        for i in range(4):
            c_ref[pl.ds(pl.multiple_of((g * 4 + i) * 8, 8), 8), :] = acc[i]
        return carry

    lax.fori_loop(0, height // 4, group, 0)
    ct_ref[...] = c_ref[...].T.astype(BF)


def side_place(i, height, breadth):
    part = lax.broadcasted_iota(jnp.int32, (8 * height, breadth), 0)
    lane = lax.broadcasted_iota(jnp.int32, (8 * height, breadth), 1)
    s = part - i * 8
    hit = ((s >= 0) & (s < 3) & (lane == s)) | ((s > 4) & (s < 8) & (lane == s + breadth - 8))
    return jnp.where(hit, 1.0, 0.0).astype(BF)


def prepare(owner, index, weight, obs_t, meta, wt_ref, p_ref, pt_ref, obs_slot, height, breadth):
    obs = wt_ref.shape[0]
    slots = p_ref.shape[0]
    n = slots // CAP
    si = lax.broadcasted_iota(jnp.int32, (obs, obs), 0)
    sj = lax.broadcasted_iota(jnp.int32, (obs, obs), 1)
    earlier = jnp.where(si < sj, 1.0, 0.0).astype(BF)
    own = owner[...]
    hot = jnp.where(lax.broadcasted_iota(jnp.int32, (n, obs), 0) == own, 1.0, 0.0)
    within = jnp.sum(nn(hot.astype(BF), earlier) * hot, axis=0, keepdims=True)
    slot_row = own * CAP + within.astype(jnp.int32)
    corner = index[0:1, :].astype(F32)
    row0 = jnp.floor((corner + 0.5) / breadth)
    meta[...] = jnp.zeros_like(meta)
    meta[0:4, :] = weight[...].astype(F32)
    meta[4:5, :] = row0
    meta[5:6, :] = corner - row0 * breadth
    meta[6:7, :] = slot_row.astype(F32)
    by_obs = meta[...].T
    w = by_obs[:, 0:4]
    whole = by_obs.astype(jnp.int32)
    lane = lax.broadcasted_iota(jnp.int32, (obs, breadth), 1)
    r0 = jnp.broadcast_to(whole[:, 4:5], (obs, breadth))
    c0 = jnp.broadcast_to(whole[:, 5:6], (obs, breadth))
    zero = jnp.zeros((obs, breadth), F32)
    first = lane == c0
    second = lane == c0 + 1
    top = jnp.where(first, w[:, 0:1], jnp.where(second, w[:, 1:2], zero))
    bottom = jnp.where(first, w[:, 2:3], jnp.where(second, w[:, 3:4], zero))
    for r in range(height):
        wt_ref[:, r * breadth : (r + 1) * breadth] = jnp.where(r0 == r, top, jnp.where(r0 == r - 1, bottom, zero)).astype(BF)
    place = lax.broadcasted_iota(jnp.int32, (slots, obs), 0) == slot_row
    p = jnp.where(place, 1.0, 0.0).astype(BF)
    p_ref[...] = p
    place = lax.broadcasted_iota(jnp.int32, (obs, slots), 1) == whole[:, 6:7]
    pt_ref[...] = jnp.where(place, 1.0, 0.0).astype(BF)
    obs_slot[...] = nt(p, obs_t[...]).astype(BF)


def remote(src, dst, send, recv, device):
    return pltpu.make_async_remote_copy(
        src_ref=src,
        dst_ref=dst,
        send_sem=send,
        recv_sem=recv,
        device_id=device,
        device_id_type=pl.DeviceIdType.MESH,
    )


def selector(breadth):
    s = lax.broadcasted_iota(jnp.int32, (8, breadth), 0)
    lane = lax.broadcasted_iota(jnp.int32, (8, breadth), 1)
    near = (s < 3) & (lane == s)
    far = (s > 4) & (lane == s + (breadth - 8))
    return jnp.where(near | far, 1.0, 0.0).astype(BF)


def copies(grid, lat_in, edge, right_in, left_in, send, recv, lats, lons):
    height = edge.shape[0]
    lat, lon = lax.axis_index("lat"), lax.axis_index("lon")
    left, right = lax.rem(lon + lons - 1, lons), lax.rem(lon + 1, lons)
    low, high, mid = pl.ds(0, 3), pl.ds(height + 3, 3), pl.ds(3, height)
    end = pl.ds(height - 3, 3)

    def make(i, a, b, device):
        return remote(a, b, send.at[i], recv.at[i], device)

    side = [
        make(2, edge, right_in.at[mid], {"lat": lat, "lon": left}),
        make(3, edge, left_in.at[mid], {"lat": lat, "lon": right}),
    ]
    u, d = lax.max(lat - 1, 0), lax.min(lat + 1, lats - 1)
    up = [
        make(0, grid.at[low], lat_in.at[1], {"lat": u, "lon": lon}),
        make(4, edge.at[low], right_in.at[high], {"lat": u, "lon": left}),
        make(5, edge.at[low], left_in.at[high], {"lat": u, "lon": right}),
    ]
    down = [
        make(1, grid.at[end], lat_in.at[0], {"lat": d, "lon": lon}),
        make(6, edge.at[end], right_in.at[low], {"lat": d, "lon": left}),
        make(7, edge.at[end], left_in.at[low], {"lat": d, "lon": right}),
    ]
    return lat > 0, lat < lats - 1, up, down, side


def start_lat(grid, lat_in, edge, right_in, left_in, send, recv, lats, lons):
    height = edge.shape[0]
    has_up, has_down, up, down, side = copies(
        grid, lat_in, edge, right_in, left_in, send, recv, lats, lons
    )

    @pl.when(has_up)
    def _():
        for copy in up:
            copy.start()

    @pl.when(has_down)
    def _():
        for copy in down:
            copy.start()

    for has, t, at in ((has_up, 0, 0), (has_down, 1, height + 3)):

        @pl.when(jnp.logical_not(has))
        def _():
            lat_in[t] = jnp.zeros(lat_in.shape[1:], BF)
            for ref in (right_in, left_in):
                ref[at : at + 3] = jnp.zeros((3,) + ref.shape[1:], BF)


def start_side(*refs):
    for copy in copies(*refs)[4]:
        copy.start()


def end_exchange(*refs):
    has_up, has_down, up, down, side = copies(*refs)

    @pl.when(has_up)
    def _():
        for copy in down:
            copy.wait_recv()
        for copy in up:
            copy.wait_send()

    @pl.when(has_down)
    def _():
        for copy in up:
            copy.wait_recv()
        for copy in down:
            copy.wait_send()

    for copy in side:
        copy.wait()


def kernel(
    lats,
    lons,
    state,
    hw_ref,
    lw_ref,
    err_ref,
    owner,
    index,
    weight,
    obs_t,
    k_ref,
    pw_ref,
    out_ref,
    dep_ref,
    cells,
    x1,
    x2,
    part,
    wide,
    w1,
    w2,
    m_sc,
    c_sc,
    ct_sc,
    lat_in,
    meta,
    tap_rows,
    taps,
    pwt,
    edge,
    right_in,
    left_in,
    ops,
    wt,
    p_mat,
    pt_mat,
    obs_slot,
    grid_f,
    ana,
    prof,
    adj,
    mis,
    send,
    recv,
    op_send,
    op_recv,
):
    channels, height, breadth = state.shape
    levels = obs_t.shape[0]
    err_row = channels + levels
    lat, lon = lax.axis_index("lat"), lax.axis_index("lon")
    partner = lon + 1 - 2 * lax.rem(lon, 2)
    other = lax.rem(lon + lons - 1 + 2 * lax.rem(lon, 2), lons)
    half = lons // 2
    bits = half.bit_length() - 1
    core, chip = lax.rem(lon, 2), lax.div(lon, 2)

    def across(q, t, c):
        first, second = flip_bit(q, 1 << t), flip_bit(q, 1 << (bits - 1 - t))
        return first + c * (second - first)

    def holder(mask, c):
        q = chip
        for t in range(bits):
            if mask >> t & 1:
                q = across(q, t, c)
        return 2 * q + c

    peers = [holder(1 << t, core) for t in range(bits)]
    barrier = pltpu.get_barrier_semaphore()

    def greet(a, b):
        pl.semaphore_signal(
            barrier,
            inc=1,
            device_id={"lat": a, "lon": b},
            device_id_type=pl.DeviceIdType.MESH,
        )

    for b in [partner, other] + peers:
        greet(lat, b)

    @pl.when(lat > 0)
    def _():
        for b in (partner, lon, other):
            greet(lat - 1, b)

    @pl.when(lat < lats - 1)
    def _():
        for b in (partner, lon, other):
            greet(lat + 1, b)

    cells[...] = state[...].reshape(channels * height, breadth).astype(F32)

    grids = (x1, x2)

    def wires(k):
        return (
            grids[k],
            lat_in.at[k],
            edge.at[k],
            right_in.at[k],
            left_in.at[k],
            send.at[k],
            recv.at[k],
            lats,
            lons,
        )

    def row_of(ref, r):
        return ref[pl.ds(r, channels, stride=height), :]

    pick = selector(breadth)

    def edge_row(r, carry):
        mine = row_of(cells, r).astype(BF)
        x1[r] = mine
        edge[0, r] = nt(pick, mine).astype(BF)
        return carry

    lax.fori_loop(0, height, edge_row, 0, unroll=8)
    ops[lon] = jnp.zeros(ops.shape[1:], BF)
    ops[lon, :channels, :] = hw_ref[0]
    ops[lon, channels : channels + levels, :] = lw_ref[0]
    ops[lon, err_row : err_row + 1, :levels] = err_ref[...]
    sides = lax.min(lat, 1) + lax.min(lats - 1 - lat, 1)
    pl.semaphore_wait(barrier, bits + 2 + 3 * sides)
    start_lat(*wires(0))
    start_side(*wires(0))
    started = []

    def op_copy(o, b):
        return remote(
            ops.at[o], ops.at[o], op_send.at[len(started)], op_recv.at[o], {"lat": lat, "lon": b}
        )

    def pass_on(mask):
        o = holder(mask, core)
        if mask:
            op_copy(o, partner).wait_recv()
        for t in range(mask.bit_length(), bits if mask else 1):
            started.append(op_copy(o, peers[t]))
            started[-1].start()
        started.append(op_copy(o, partner))
        started[-1].start()

    pass_on(0)
    tap_rows[...] = jnp.zeros_like(tap_rows)
    for row in range(7):
        tap_rows[8 * row : 8 * row + 7, :] = k_ref[row].astype(F32)
    taps[...] = tap_rows[...].T
    pwt[...] = pw_ref[...].astype(F32).T.astype(BF)

    def group(g, carry):
        base = pl.multiple_of(g * 16, 16)
        local = taps[pl.ds(base, 16), :]

        def spread(col):
            out = []
            for row in range(7):
                t = row * 8 + col
                w = jnp.broadcast_to(local[:, t : t + 1], (16, breadth))
                wide[g, row * 7 + col] = w
                out.append(w.astype(BF))
            return out

        conv_own(x1, part, spread, base)
        return carry

    lax.fori_loop(0, channels // 16, group, 0)

    def straight(g):
        return lambda col: [wide[g, row * 7 + col].astype(BF) for row in range(7)]

    def flipped(g):
        return lambda col: [wide[g, (6 - row) * 7 + 6 - col].astype(BF) for row in range(7)]

    for t in range(1, bits):
        started.append(op_copy(lon, peers[t]))
        started[-1].start()
    side_weights(k_ref, False, w1)
    prepare(
        owner, index, weight, obs_t, meta, wt, p_mat, pt_mat, obs_slot, height, breadth
    )
    end_exchange(*wires(0))
    side_sum(right_in.at[0], left_in.at[0], w1, m_sc, c_sc, ct_sc)

    def add_edge(g, carry):
        conv_edge(lat_in.at[0], part, straight(g), pl.multiple_of(g * 16, 16))
        return carry

    lax.fori_loop(0, channels // 16, add_edge, 0, unroll=2)
    pass_on(1)

    side_weights(k_ref, True, w2)
    a, c3 = 0.7978845608028654, 0.044715

    def ahead(q, carry):
        r = q * 2
        place = [side_place(r + t, height, breadth) for t in range(2)]
        side = nn(ct_sc[...], jnp.concatenate(place, axis=1))
        mixed = jnp.concatenate([part[r], part[r + 1]], axis=1) + side
        pre = nn(pwt[...], mixed.astype(BF))
        square = pre * pre
        t = jnp.tanh(a * (pre + c3 * (square * pre)))
        gate = 0.5 * (1.0 + t)
        slope = gate + (0.5 * pre) * (1.0 - t * t) * (a * (1.0 + (3.0 * c3) * square))
        two = pl.ds(pl.multiple_of(q * 2 * breadth, 2 * breadth), 2 * breadth)
        grid_f[:, two] = slope
        here = jnp.concatenate([x1[r], x1[r + 1]], axis=1).astype(F32)
        ana[:, two] = (here + pre * gate).astype(BF)
        return carry

    lax.fori_loop(0, height // 4, ahead, 0, unroll=2)
    lax.fori_loop(height // 4, height // 2, ahead, 0, unroll=2)
    total = nt(wt[...], ana[...])
    prof[...] = nn(p_mat[...], total.astype(BF)).astype(BF)

    def instrument(o):
        at = pl.ds(pl.multiple_of(o * CAP, CAP), CAP)
        hw = ops[o, :channels, :]
        lw = ops[o, channels : channels + levels, :]
        err = ops[o, err_row : err_row + 1, :levels].astype(F32)
        squashed = jnp.tanh(nn(prof[at, :], hw))
        misfit = nt(squashed.astype(BF), lw) - obs_slot[at, :].astype(F32)
        mis[at, :] = misfit.astype(BF)
        back = nn((err * misfit).astype(BF), lw) * (1.0 - squashed * squashed)
        adj[at, :] = nt(back.astype(BF), hw).astype(BF)

    def from_partner(mask):
        o = holder(mask, 1 - core)
        op_copy(o, partner).wait_recv()
        return o

    for mask in range(2, half - 1):
        pass_on(mask)
    early = [lon, from_partner(0)] + [holder(mask, core) for mask in range(1, half - 1)]
    for o in early:
        instrument(o)
    if half > 2:
        pass_on(half - 1)
    late = [from_partner(mask) for mask in range(1, half)]
    for o in [holder(half - 1, core)] + late:
        instrument(o)
    dep_ref[...] = nn(pt_mat[...], mis[...]).T.astype(BF)
    adj_t = nn(pt_mat[...], adj[...]).T.astype(BF)

    def behind(q, carry):
        r = q * 2
        two = pl.ds(pl.multiple_of(q * 2 * breadth, 2 * breadth), 2 * breadth)
        fb = nn(adj_t, wt[:, two])
        gate = (fb * grid_f[:, two]).astype(BF)
        grid_f[:, two] = fb
        mb = nn(pw_ref[...], gate).astype(BF)
        for t in range(2):
            mine = mb[:, t * breadth : (t + 1) * breadth]
            x2[r + t] = mine
            edge[1, r + t] = nt(pick, mine).astype(BF)
        return carry

    last = height // 2
    lax.fori_loop(0, 2, behind, 0, unroll=2)
    lax.fori_loop(last - 2, last, behind, 0, unroll=2)
    start_lat(*wires(1))
    lax.fori_loop(2, last - 2, behind, 0, unroll=2)
    start_side(*wires(1))

    def group_back(g, carry):
        conv_own(x2, part, flipped(g), pl.multiple_of(g * 16, 16))
        return carry

    lax.fori_loop(0, channels // 16, group_back, 0)
    for copy in started:
        copy.wait_send()
    end_exchange(*wires(1))
    side_sum(right_in.at[1], left_in.at[1], w2, m_sc, c_sc, ct_sc)

    def edge_back(g, carry):
        conv_edge(lat_in.at[1], part, flipped(g), pl.multiple_of(g * 16, 16))
        return carry

    lax.fori_loop(0, channels // 16, edge_back, 0, unroll=2)

    def add_side(q, carry):
        r = q * 2
        two = pl.ds(pl.multiple_of(q * 2 * breadth, 2 * breadth), 2 * breadth)
        place = [side_place(r + t, height, breadth) for t in range(2)]
        side = nn(ct_sc[...], jnp.concatenate(place, axis=1)) + grid_f[:, two]
        for t in range(2):
            cells[pl.ds(r + t, channels, stride=height), :] = (
                side[:, t * breadth : (t + 1) * breadth] + part[r + t]
            )
        return carry

    lax.fori_loop(0, height // 2, add_side, 0, unroll=2)
    out_ref[...] = cells[...].astype(BF).reshape(out_ref.shape)


def body(
    state,
    depth_kernel,
    point_weight,
    column_index,
    column_weight,
    owner,
    observed,
    hidden_weight,
    level_weight,
    inverse_error,
):
    channels, height, breadth = state.shape
    obs, levels = observed.shape
    hid = hidden_weight.shape[2]
    lats, n = lax.axis_size("lat"), lax.axis_size("lon")
    slots = n * CAP
    depth = channels + levels + 1 + (-(channels + levels + 1)) % 16
    args = (
        state,
        hidden_weight,
        level_weight.transpose(0, 2, 1),
        inverse_error,
        owner.T,
        column_index.T,
        column_weight.T,
        observed.T,
        depth_kernel.transpose(1, 2, 0),
        point_weight,
    )
    rows = height + 6
    vm = pltpu.VMEM
    grad, departures = pl.pallas_call(
        lambda *refs: kernel(lats, n, *refs),
        out_shape=(
            jax.ShapeDtypeStruct((channels, height, breadth), BF),
            jax.ShapeDtypeStruct((levels, obs), BF),
        ),
        in_specs=[VM] * len(args),
        out_specs=(VM, VM),
        scratch_shapes=[
            vm((channels * height, breadth), F32),
            vm((height, channels, breadth), BF),
            vm((height, channels, breadth), BF),
            vm((height, channels, breadth), F32),
            vm((channels // 16, 49, 16, breadth), F32),
            vm((21, 8, channels), F32),
            vm((21, 8, channels), F32),
            vm((3, rows, 8, channels), F32),
            vm((8 * height, channels), F32),
            vm((channels, 8 * height), BF),
            vm((2, 2, 3, channels, breadth), BF),
            vm((8, obs), F32),
            vm((64, channels), F32),
            vm((channels, 64), F32),
            vm((channels, channels), BF),
            vm((2, height, 8, channels), BF),
            vm((2, rows, 8, channels), BF),
            vm((2, rows, 8, channels), BF),
            vm((n, depth, hid), BF),
            vm((obs, height * breadth), BF),
            vm((slots, obs), BF),
            vm((obs, slots), BF),
            vm((slots, levels), BF),
            vm((channels, height * breadth), F32),
            vm((channels, height * breadth), BF),
            vm((slots, channels), BF),
            vm((slots, channels), BF),
            vm((slots, levels), BF),
            pltpu.SemaphoreType.DMA((2, 8)),
            pltpu.SemaphoreType.DMA((2, 8)),
            pltpu.SemaphoreType.DMA((n,)),
            pltpu.SemaphoreType.DMA((n,)),
        ],
        compiler_params=pltpu.CompilerParams(
            vmem_limit_bytes=56 << 20, collective_id=0, has_side_effects=True
        ),
    )(*args)
    return (grad, departures.T)


def solution(mesh):
    in_specs = (
        P(None, "lat", "lon"),
        P(),
        P(),
        P(("lat", "lon"), None),
        P(("lat", "lon"), None),
        P(("lat", "lon"), None),
        P(("lat", "lon"), None),
        P("lon", None, None),
        P("lon", None, None),
        P("lon", None),
    )
    out_specs = (P(None, "lat", "lon"), P(("lat", "lon"), None))
    return jax.shard_map(body, mesh=mesh, in_specs=in_specs, out_specs=out_specs, check_vma=False)
```

```python
import jax
import jax.numpy as jnp
from jax import lax
from jax.experimental import pallas as pl
from jax.experimental.pallas import tpu as pltpu
from jax.sharding import PartitionSpec as P

CAP = 64
F32 = jnp.float32
BF = jnp.bfloat16
VM = pl.BlockSpec(memory_space=pltpu.VMEM)


def nn(a, b):
    return jnp.dot(a, b, preferred_element_type=F32)


def nt(a, b):
    return lax.dot_general(a, b, (((1,), (1,)), ((), ())), preferred_element_type=F32)


def flip_bit(q, bit):
    return q + bit * (1 - 2 * lax.rem(lax.div(q, bit), 2))


def shifted(v, shift):
    breadth = v.shape[1]
    if not shift:
        return v
    lane = lax.broadcasted_iota(jnp.int32, v.shape, 1)
    keep = lane < breadth - shift if shift > 0 else lane >= -shift
    return jnp.where(keep, pltpu.roll(v, (-shift) % breadth, 1), jnp.zeros_like(v))


def side_weights(k_ref, flip, w_ref):
    channels = k_ref.shape[2]
    slot = lax.broadcasted_iota(jnp.int32, (8, channels), 0)
    for a in range(7):
        taps = k_ref[6 - a if flip else a].astype(F32)
        for d in range(3):
            r, l = (d, 6 - d) if flip else (6 - d, d)
            right = jnp.where(slot >= 5 + d, jnp.broadcast_to(taps[r : r + 1], slot.shape), 0.0)
            left = jnp.where(slot <= 2 - d, jnp.broadcast_to(taps[l : l + 1], slot.shape), 0.0)
            w_ref[a * 3 + d] = right + left


def conv_own(x, out, weights, base):
    height, _, breadth = x.shape
    at = pl.ds(base, 16)
    acc = [None] * height
    for col in range(7):
        w = weights(col)
        part = [None] * height
        for r in range(height):
            v = shifted(x[r, at, :], col - 3)
            for row in range(7):
                i = r + 3 - row
                if 0 <= i < height:
                    term = w[row] * v
                    part[i] = term if part[i] is None else part[i] + term
            for i in range(height):
                if part[i] is not None and r == min(i + 3, height - 1):
                    whole = part[i].astype(F32)
                    acc[i] = whole if acc[i] is None else acc[i] + whole
                    part[i] = None
    for i in range(height):
        out[i, at, :] = acc[i]


def conv_edge(lat_in, out, weights, base):
    height = out.shape[0]
    at = pl.ds(base, 16)
    acc = {}
    for col in range(7):
        w = weights(col)
        part = {}
        for t in range(2):
            for k in range(3):
                v = shifted(lat_in[t, k, at, :], col - 3)
                span = range(0, k + 1) if t == 0 else range(height - 3 + k, height)
                for i in span:
                    term = w[k - i if t == 0 else height + 3 + k - i] * v
                    part[i] = part[i] + term if i in part else term
        for i, v in part.items():
            whole = v.astype(F32)
            acc[i] = acc[i] + whole if i in acc else whole
    for i, v in acc.items():
        out[i, at, :] = out[i, at, :] + v


def side_sum(right_in, left_in, w_ref, m_ref, c_ref, ct_ref):
    rows, _, channels = right_in.shape
    height = rows - 6
    slot = lax.broadcasted_iota(jnp.int32, (8, channels), 0)

    def turn(r, carry):
        both = jnp.where(slot < 4, right_in[r].astype(F32), left_in[r].astype(F32))
        for d in range(3):
            m_ref[d, r] = jnp.where(
                slot >= 5, pltpu.roll(both, 5 + d, 0), pltpu.roll(both, 3 - d, 0)
            )
        return carry

    lax.fori_loop(0, rows, turn, 0, unroll=2)

    def group(g, carry):
        acc = [jnp.zeros((8, channels), F32) for _ in range(4)]
        for d in range(3):
            for a in range(7):
                w = w_ref[a * 3 + d]
                for i in range(4):
                    acc[i] = acc[i] + w * m_ref[d, g * 4 + i + a]
        for i in range(4):
            c_ref[pl.ds(pl.multiple_of((g * 4 + i) * 8, 8), 8), :] = acc[i]
        return carry

    lax.fori_loop(0, height // 4, group, 0)
    ct_ref[...] = c_ref[...].T.astype(BF)


def side_place(i, height, breadth):
    part = lax.broadcasted_iota(jnp.int32, (8 * height, breadth), 0)
    lane = lax.broadcasted_iota(jnp.int32, (8 * height, breadth), 1)
    s = part - i * 8
    hit = ((s >= 0) & (s < 3) & (lane == s)) | ((s > 4) & (s < 8) & (lane == s + breadth - 8))
    return jnp.where(hit, 1.0, 0.0).astype(BF)


def prepare(owner, index, weight, obs_t, meta, wt_ref, p_ref, pt_ref, obs_slot, height, breadth):
    obs = wt_ref.shape[0]
    slots = p_ref.shape[0]
    n = slots // CAP
    si = lax.broadcasted_iota(jnp.int32, (obs, obs), 0)
    sj = lax.broadcasted_iota(jnp.int32, (obs, obs), 1)
    earlier = jnp.where(si < sj, 1.0, 0.0).astype(BF)
    own = owner[...]
    hot = jnp.where(lax.broadcasted_iota(jnp.int32, (n, obs), 0) == own, 1.0, 0.0)
    within = jnp.sum(nn(hot.astype(BF), earlier) * hot, axis=0, keepdims=True)
    slot_row = own * CAP + within.astype(jnp.int32)
    corner = index[0:1, :].astype(F32)
    row0 = jnp.floor((corner + 0.5) / breadth)
    meta[...] = jnp.zeros_like(meta)
    meta[0:4, :] = weight[...].astype(F32)
    meta[4:5, :] = row0
    meta[5:6, :] = corner - row0 * breadth
    meta[6:7, :] = slot_row.astype(F32)
    by_obs = meta[...].T
    w = by_obs[:, 0:4]
    whole = by_obs.astype(jnp.int32)
    lane = lax.broadcasted_iota(jnp.int32, (obs, breadth), 1)
    r0 = jnp.broadcast_to(whole[:, 4:5], (obs, breadth))
    c0 = jnp.broadcast_to(whole[:, 5:6], (obs, breadth))
    zero = jnp.zeros((obs, breadth), F32)
    first = lane == c0
    second = lane == c0 + 1
    top = jnp.where(first, w[:, 0:1], jnp.where(second, w[:, 1:2], zero))
    bottom = jnp.where(first, w[:, 2:3], jnp.where(second, w[:, 3:4], zero))
    for r in range(height):
        wt_ref[:, r * breadth : (r + 1) * breadth] = jnp.where(r0 == r, top, jnp.where(r0 == r - 1, bottom, zero)).astype(BF)
    place = lax.broadcasted_iota(jnp.int32, (slots, obs), 0) == slot_row
    p = jnp.where(place, 1.0, 0.0).astype(BF)
    p_ref[...] = p
    place = lax.broadcasted_iota(jnp.int32, (obs, slots), 1) == whole[:, 6:7]
    pt_ref[...] = jnp.where(place, 1.0, 0.0).astype(BF)
    obs_slot[...] = nt(p, obs_t[...]).astype(BF)


def remote(src, dst, send, recv, device):
    return pltpu.make_async_remote_copy(
        src_ref=src,
        dst_ref=dst,
        send_sem=send,
        recv_sem=recv,
        device_id=device,
        device_id_type=pl.DeviceIdType.MESH,
    )


def selector(breadth):
    s = lax.broadcasted_iota(jnp.int32, (8, breadth), 0)
    lane = lax.broadcasted_iota(jnp.int32, (8, breadth), 1)
    near = (s < 3) & (lane == s)
    far = (s > 4) & (lane == s + (breadth - 8))
    return jnp.where(near | far, 1.0, 0.0).astype(BF)


def copies(grid, lat_in, edge, right_in, left_in, send, recv, lats, lons):
    height = edge.shape[0]
    lat, lon = lax.axis_index("lat"), lax.axis_index("lon")
    left, right = lax.rem(lon + lons - 1, lons), lax.rem(lon + 1, lons)
    low, high, mid = pl.ds(0, 3), pl.ds(height + 3, 3), pl.ds(3, height)
    end = pl.ds(height - 3, 3)

    def make(i, a, b, device):
        return remote(a, b, send.at[i], recv.at[i], device)

    side = [
        make(2, edge, right_in.at[mid], {"lat": lat, "lon": left}),
        make(3, edge, left_in.at[mid], {"lat": lat, "lon": right}),
    ]
    u, d = lax.max(lat - 1, 0), lax.min(lat + 1, lats - 1)
    up = [
        make(0, grid.at[low], lat_in.at[1], {"lat": u, "lon": lon}),
        make(4, edge.at[low], right_in.at[high], {"lat": u, "lon": left}),
        make(5, edge.at[low], left_in.at[high], {"lat": u, "lon": right}),
    ]
    down = [
        make(1, grid.at[end], lat_in.at[0], {"lat": d, "lon": lon}),
        make(6, edge.at[end], right_in.at[low], {"lat": d, "lon": left}),
        make(7, edge.at[end], left_in.at[low], {"lat": d, "lon": right}),
    ]
    return lat > 0, lat < lats - 1, up, down, side


def start_lat(grid, lat_in, edge, right_in, left_in, send, recv, lats, lons):
    height = edge.shape[0]
    has_up, has_down, up, down, side = copies(
        grid, lat_in, edge, right_in, left_in, send, recv, lats, lons
    )

    @pl.when(has_up)
    def _():
        for copy in up:
            copy.start()

    @pl.when(has_down)
    def _():
        for copy in down:
            copy.start()

    for has, t, at in ((has_up, 0, 0), (has_down, 1, height + 3)):

        @pl.when(jnp.logical_not(has))
        def _():
            lat_in[t] = jnp.zeros(lat_in.shape[1:], BF)
            for ref in (right_in, left_in):
                ref[at : at + 3] = jnp.zeros((3,) + ref.shape[1:], BF)


def start_side(*refs):
    for copy in copies(*refs)[4]:
        copy.start()


def end_exchange(*refs):
    has_up, has_down, up, down, side = copies(*refs)

    @pl.when(has_up)
    def _():
        for copy in down:
            copy.wait_recv()
        for copy in up:
            copy.wait_send()

    @pl.when(has_down)
    def _():
        for copy in up:
            copy.wait_recv()
        for copy in down:
            copy.wait_send()

    for copy in side:
        copy.wait()


def kernel(
    lats,
    lons,
    state,
    hw_ref,
    lw_ref,
    err_ref,
    owner,
    index,
    weight,
    obs_t,
    k_ref,
    pw_ref,
    out_ref,
    dep_ref,
    cells,
    x1,
    x2,
    part,
    wide,
    w1,
    w2,
    m_sc,
    c_sc,
    ct_sc,
    lat_in,
    meta,
    tap_rows,
    taps,
    pwt,
    edge,
    right_in,
    left_in,
    ops,
    wt,
    p_mat,
    pt_mat,
    obs_slot,
    grid_f,
    ana,
    prof,
    adj,
    mis,
    send,
    recv,
    op_send,
    op_recv,
):
    channels, height, breadth = state.shape
    levels = obs_t.shape[0]
    err_row = channels + levels
    lat, lon = lax.axis_index("lat"), lax.axis_index("lon")
    partner = lon + 1 - 2 * lax.rem(lon, 2)
    other = lax.rem(lon + lons - 1 + 2 * lax.rem(lon, 2), lons)
    half = lons // 2
    bits = half.bit_length() - 1
    core, chip = lax.rem(lon, 2), lax.div(lon, 2)

    def across(q, t, c):
        first, second = flip_bit(q, 1 << t), flip_bit(q, 1 << (bits - 1 - t))
        return first + c * (second - first)

    def holder(mask, c):
        q = chip
        for t in range(bits):
            if mask >> t & 1:
                q = across(q, t, c)
        return 2 * q + c

    peers = [holder(1 << t, core) for t in range(bits)]
    barrier = pltpu.get_barrier_semaphore()

    def greet(a, b):
        pl.semaphore_signal(
            barrier,
            inc=1,
            device_id={"lat": a, "lon": b},
            device_id_type=pl.DeviceIdType.MESH,
        )

    for b in [partner, other] + peers:
        greet(lat, b)

    @pl.when(lat > 0)
    def _():
        for b in (partner, lon, other):
            greet(lat - 1, b)

    @pl.when(lat < lats - 1)
    def _():
        for b in (partner, lon, other):
            greet(lat + 1, b)

    cells[...] = state[...].reshape(channels * height, breadth).astype(F32)

    grids = (x1, x2)

    def wires(k):
        return (
            grids[k],
            lat_in.at[k],
            edge.at[k],
            right_in.at[k],
            left_in.at[k],
            send.at[k],
            recv.at[k],
            lats,
            lons,
        )

    def row_of(ref, r):
        return ref[pl.ds(r, channels, stride=height), :]

    pick = selector(breadth)

    def edge_row(r, carry):
        mine = row_of(cells, r).astype(BF)
        x1[r] = mine
        edge[0, r] = nt(pick, mine).astype(BF)
        return carry

    lax.fori_loop(0, height, edge_row, 0, unroll=8)
    ops[lon] = jnp.zeros(ops.shape[1:], BF)
    ops[lon, :channels, :] = hw_ref[0]
    ops[lon, channels : channels + levels, :] = lw_ref[0]
    ops[lon, err_row : err_row + 1, :levels] = err_ref[...]
    sides = lax.min(lat, 1) + lax.min(lats - 1 - lat, 1)
    pl.semaphore_wait(barrier, bits + 2 + 3 * sides)
    start_lat(*wires(0))
    start_side(*wires(0))
    started = []

    def op_copy(o, b):
        return remote(
            ops.at[o], ops.at[o], op_send.at[len(started)], op_recv.at[o], {"lat": lat, "lon": b}
        )

    def pass_on(mask):
        o = holder(mask, core)
        if mask:
            op_copy(o, partner).wait_recv()
        for t in range(mask.bit_length(), bits if mask else 1):
            started.append(op_copy(o, peers[t]))
            started[-1].start()
        started.append(op_copy(o, partner))
        started[-1].start()

    pass_on(0)
    tap_rows[...] = jnp.zeros_like(tap_rows)
    for row in range(7):
        tap_rows[8 * row : 8 * row + 7, :] = k_ref[row].astype(F32)
    taps[...] = tap_rows[...].T
    pwt[...] = pw_ref[...].astype(F32).T.astype(BF)

    def group(g, carry):
        base = pl.multiple_of(g * 16, 16)
        local = taps[pl.ds(base, 16), :]

        def spread(col):
            out = []
            for row in range(7):
                t = row * 8 + col
                w = jnp.broadcast_to(local[:, t : t + 1], (16, breadth))
                wide[g, row * 7 + col] = w
                out.append(w.astype(BF))
            return out

        conv_own(x1, part, spread, base)
        return carry

    lax.fori_loop(0, channels // 16, group, 0)

    def straight(g):
        return lambda col: [wide[g, row * 7 + col].astype(BF) for row in range(7)]

    def flipped(g):
        return lambda col: [wide[g, (6 - row) * 7 + 6 - col].astype(BF) for row in range(7)]

    for t in range(1, bits):
        started.append(op_copy(lon, peers[t]))
        started[-1].start()
    side_weights(k_ref, False, w1)
    prepare(
        owner, index, weight, obs_t, meta, wt, p_mat, pt_mat, obs_slot, height, breadth
    )
    end_exchange(*wires(0))
    side_sum(right_in.at[0], left_in.at[0], w1, m_sc, c_sc, ct_sc)

    def add_edge(g, carry):
        conv_edge(lat_in.at[0], part, straight(g), pl.multiple_of(g * 16, 16))
        return carry

    lax.fori_loop(0, channels // 16, add_edge, 0, unroll=2)
    pass_on(1)

    side_weights(k_ref, True, w2)
    a, c3 = 0.7978845608028654, 0.044715

    def ahead(q, carry):
        r = q * 2
        place = [side_place(r + t, height, breadth) for t in range(2)]
        side = nn(ct_sc[...], jnp.concatenate(place, axis=1))
        mixed = jnp.concatenate([part[r], part[r + 1]], axis=1) + side
        pre = nn(pwt[...], mixed.astype(BF))
        square = pre * pre
        t = jnp.tanh(a * (pre + c3 * (square * pre)))
        gate = 0.5 * (1.0 + t)
        slope = gate + (0.5 * pre) * (1.0 - t * t) * (a * (1.0 + (3.0 * c3) * square))
        two = pl.ds(pl.multiple_of(q * 2 * breadth, 2 * breadth), 2 * breadth)
        grid_f[:, two] = slope
        here = jnp.concatenate([x1[r], x1[r + 1]], axis=1).astype(F32)
        ana[:, two] = (here + pre * gate).astype(BF)
        return carry

    lax.fori_loop(0, height // 4, ahead, 0, unroll=2)
    lax.fori_loop(height // 4, height // 2, ahead, 0, unroll=2)
    total = nt(wt[...], ana[...])
    prof[...] = nn(p_mat[...], total.astype(BF)).astype(BF)

    def instrument(o):
        at = pl.ds(pl.multiple_of(o * CAP, CAP), CAP)
        hw = ops[o, :channels, :]
        lw = ops[o, channels : channels + levels, :]
        err = ops[o, err_row : err_row + 1, :levels].astype(F32)
        squashed = jnp.tanh(nn(prof[at, :], hw))
        misfit = nt(squashed.astype(BF), lw) - obs_slot[at, :].astype(F32)
        mis[at, :] = misfit.astype(BF)
        back = nn((err * misfit).astype(BF), lw) * (1.0 - squashed * squashed)
        adj[at, :] = nt(back.astype(BF), hw).astype(BF)

    def from_partner(mask):
        o = holder(mask, 1 - core)
        op_copy(o, partner).wait_recv()
        return o

    for mask in range(2, half - 1):
        pass_on(mask)
    early = [lon, from_partner(0)] + [holder(mask, core) for mask in range(1, half - 1)]
    for o in early:
        instrument(o)
    if half > 2:
        pass_on(half - 1)
    late = [from_partner(mask) for mask in range(1, half)]
    for o in [holder(half - 1, core)] + late:
        instrument(o)
    dep_ref[...] = nn(pt_mat[...], mis[...]).T.astype(BF)
    adj_t = nn(pt_mat[...], adj[...]).T.astype(BF)

    def behind(q, carry):
        r = q * 2
        two = pl.ds(pl.multiple_of(q * 2 * breadth, 2 * breadth), 2 * breadth)
        fb = nn(adj_t, wt[:, two])
        gate = (fb * grid_f[:, two]).astype(BF)
        grid_f[:, two] = fb
        mb = nn(pw_ref[...], gate).astype(BF)
        for t in range(2):
            mine = mb[:, t * breadth : (t + 1) * breadth]
            x2[r + t] = mine
            edge[1, r + t] = nt(pick, mine).astype(BF)
        return carry

    last = height // 2
    lax.fori_loop(0, 2, behind, 0, unroll=2)
    lax.fori_loop(last - 2, last, behind, 0, unroll=2)
    start_lat(*wires(1))
    lax.fori_loop(2, last - 2, behind, 0, unroll=2)
    start_side(*wires(1))

    def group_back(g, carry):
        conv_own(x2, part, flipped(g), pl.multiple_of(g * 16, 16))
        return carry

    lax.fori_loop(0, channels // 16, group_back, 0)
    for copy in started:
        copy.wait_send()
    end_exchange(*wires(1))
    side_sum(right_in.at[1], left_in.at[1], w2, m_sc, c_sc, ct_sc)

    def edge_back(g, carry):
        conv_edge(lat_in.at[1], part, flipped(g), pl.multiple_of(g * 16, 16))
        return carry

    lax.fori_loop(0, channels // 16, edge_back, 0, unroll=4)

    def add_side(q, carry):
        r = q * 2
        two = pl.ds(pl.multiple_of(q * 2 * breadth, 2 * breadth), 2 * breadth)
        place = [side_place(r + t, height, breadth) for t in range(2)]
        side = nn(ct_sc[...], jnp.concatenate(place, axis=1)) + grid_f[:, two]
        for t in range(2):
            cells[pl.ds(r + t, channels, stride=height), :] = (
                side[:, t * breadth : (t + 1) * breadth] + part[r + t]
            )
        return carry

    lax.fori_loop(0, height // 2, add_side, 0, unroll=4)
    out_ref[...] = cells[...].astype(BF).reshape(out_ref.shape)


def body(
    state,
    depth_kernel,
    point_weight,
    column_index,
    column_weight,
    owner,
    observed,
    hidden_weight,
    level_weight,
    inverse_error,
):
    channels, height, breadth = state.shape
    obs, levels = observed.shape
    hid = hidden_weight.shape[2]
    lats, n = lax.axis_size("lat"), lax.axis_size("lon")
    slots = n * CAP
    depth = channels + levels + 1 + (-(channels + levels + 1)) % 16
    args = (
        state,
        hidden_weight,
        level_weight.transpose(0, 2, 1),
        inverse_error,
        owner.T,
        column_index.T,
        column_weight.T,
        observed.T,
        depth_kernel.transpose(1, 2, 0),
        point_weight,
    )
    rows = height + 6
    vm = pltpu.VMEM
    grad, departures = pl.pallas_call(
        lambda *refs: kernel(lats, n, *refs),
        out_shape=(
            jax.ShapeDtypeStruct((channels, height, breadth), BF),
            jax.ShapeDtypeStruct((levels, obs), BF),
        ),
        in_specs=[VM] * len(args),
        out_specs=(VM, VM),
        scratch_shapes=[
            vm((channels * height, breadth), F32),
            vm((height, channels, breadth), BF),
            vm((height, channels, breadth), BF),
            vm((height, channels, breadth), F32),
            vm((channels // 16, 49, 16, breadth), F32),
            vm((21, 8, channels), F32),
            vm((21, 8, channels), F32),
            vm((3, rows, 8, channels), F32),
            vm((8 * height, channels), F32),
            vm((channels, 8 * height), BF),
            vm((2, 2, 3, channels, breadth), BF),
            vm((8, obs), F32),
            vm((64, channels), F32),
            vm((channels, 64), F32),
            vm((channels, channels), BF),
            vm((2, height, 8, channels), BF),
            vm((2, rows, 8, channels), BF),
            vm((2, rows, 8, channels), BF),
            vm((n, depth, hid), BF),
            vm((obs, height * breadth), BF),
            vm((slots, obs), BF),
            vm((obs, slots), BF),
            vm((slots, levels), BF),
            vm((channels, height * breadth), F32),
            vm((channels, height * breadth), BF),
            vm((slots, channels), BF),
            vm((slots, channels), BF),
            vm((slots, levels), BF),
            pltpu.SemaphoreType.DMA((2, 8)),
            pltpu.SemaphoreType.DMA((2, 8)),
            pltpu.SemaphoreType.DMA((n,)),
            pltpu.SemaphoreType.DMA((n,)),
        ],
        compiler_params=pltpu.CompilerParams(
            vmem_limit_bytes=56 << 20, collective_id=0, has_side_effects=True
        ),
    )(*args)
    return (grad, departures.T)


def solution(mesh):
    in_specs = (
        P(None, "lat", "lon"),
        P(),
        P(),
        P(("lat", "lon"), None),
        P(("lat", "lon"), None),
        P(("lat", "lon"), None),
        P(("lat", "lon"), None),
        P("lon", None, None),
        P("lon", None, None),
        P("lon", None),
    )
    out_specs = (P(None, "lat", "lon"), P(("lat", "lon"), None))
    return jax.shard_map(body, mesh=mesh, in_specs=in_specs, out_specs=out_specs, check_vma=False)
```
